256 devices in a mesh: grp: 2 (over y_hi), ta: 8 (over y_lo, x), xyz: 16 (over z, core).
Axes of the slice: x: 4, y: 4 (y_hi: 2, y_lo: 2; y = y_hi * 2 + y_lo), z: 8, core: 2. Of those that a mesh axis runs over, the one named last changes fastest.
Arguments:
- right_sides: float32 [4, 24, 8, 32, 256], P('grp', None, 'ta', 'xyz'), may hold values from -6 to 6
- gauge_links: float32 [4, 18, 8, 32, 256], P(None, None, 'ta', 'xyz'), may hold values from -1.8 to 1.8
- eigenvectors: bfloat16 [8, 256, 6, 32, 256], P('ta', 'grp', None, 'xyz'), may hold values from -6 to 6
- step_lengths: float32 [4], replicated, may hold values from 0.6 to 1
Outputs:
- solution: float32 [4, 24, 8, 32, 256], P('grp', None, 'ta', 'xyz')
- correlations: float32 [8, 256, 3, 2, 256], P('ta', 'xyz', None, None, 'grp')
- perambulator: float32 [8, 256, 4, 8], P('ta', 'xyz', 'grp')
The draws below stay inside these ranges and needn't reach their ends.
All inputs are finite; a program needn't handle non-finite values.
Results may differ from the reference program's by a relative error of at most 0.0029.
Values may be sent and summed in bfloat16 or wider, within the bound.
A program may use at most 128 MiB of HBM per device.

```python
import math
import jax
import jax.numpy as jnp
from jax import lax

NEV = 256
RHS = 4
SX = 16
ITERS = 4
NZ = 32
NT = 8


def steps_of(own_key, shape, cuts, smallest, high):
    def one(position, shards_of):
        draws = jax.random.uniform(jax.random.fold_in(jax.random.fold_in(own_key, 6), position), (shards_of,), jnp.float32, smallest / len(cuts), high / len(cuts))
        return jnp.repeat(jnp.exp(draws), shape[position] // shards_of).reshape((-1,) + (1,) * (len(shape) - position - 1))

    gain = one(*cuts[0])
    for cut in cuts[1:]:
        gain = gain * one(*cut)
    return gain


def gaussian(own_key, shape, deviation, reach, cuts=(), kind=jnp.bfloat16):
    result = deviation * jax.random.normal(own_key, shape, jnp.float32)
    if cuts:
        result = result * steps_of(own_key, shape, cuts, -0.22, 0.18)
    return jnp.clip(result, -reach, reach).astype(kind)


def setup_inputs(seed: int = 0) -> dict:
    key_of = jax.random.split(jax.random.key(seed), 5)
    right_sides = gaussian(key_of[0], (RHS, 24, NT, NZ, SX * SX), 1.0, 6.0, ((0, 2), (2, 8), (3, 16)), jnp.float32)
    gauge_links = gaussian(key_of[1], (4, 18, NT, NZ, SX * SX), 0.3, 1.8, ((2, 8), (3, 16)), jnp.float32)
    eigenvectors = gaussian(key_of[2], (NT, NEV, 6, NZ, SX * SX), 1.0, 6.0, ((0, 8), (1, 2), (3, 16)))
    step_lengths = jnp.clip(jax.random.uniform(key_of[3], (ITERS,), jnp.float32, 0.6, 1.0), 0.6, 1.0)
    return dict(right_sides=right_sides, gauge_links=gauge_links, eigenvectors=eigenvectors, step_lengths=step_lengths)


HOPPING = 0.1
GAMMA_TABLE = (((3, 0.0, 1.0), (2, 0.0, 1.0), (1, 0.0, -1.0), (0, 0.0, -1.0)), ((3, -1.0, 0.0), (2, 1.0, 0.0), (1, 1.0, 0.0), (0, -1.0, 0.0)), ((2, 0.0, 1.0), (3, 0.0, -1.0), (0, 0.0, -1.0), (1, 0.0, 1.0)), ((2, 1.0, 0.0), (3, 1.0, 0.0), (0, 1.0, 0.0), (1, 1.0, 0.0)))

def along_x(values, offset, row_width):
    column = jnp.arange(values.shape[-1]) % row_width
    if offset > 0:
        return jnp.where(column == row_width - 1, jnp.roll(values, row_width - 1, axis=-1), jnp.roll(values, -1, axis=-1))
    return jnp.where(column == 0, jnp.roll(values, 1 - row_width, axis=-1), jnp.roll(values, 1, axis=-1))

def along_y(values, offset, row_width):
    return jnp.roll(values, -offset * row_width, axis=-1)

def gamma_apply(spinor, direction):
    spin_rows = []
    for target in range(4):
        source, real_phase, imag_phase = GAMMA_TABLE[direction][target]
        real_part = spinor[:, source, 0]
        imag_part = spinor[:, source, 1]
        spin_rows.append(jnp.stack([real_phase * real_part - imag_phase * imag_part, real_phase * imag_part + imag_phase * real_part], axis=1))
    return jnp.stack(spin_rows, axis=1)

def link_lists(link_field):
    real_rows = [[link_field[3 * target + source] for source in range(3)] for target in range(3)]
    imag_rows = [[link_field[9 + 3 * target + source] for source in range(3)] for target in range(3)]
    return (real_rows, imag_rows)

def colour_apply(link_parts, real_vec, imag_vec, dagger):
    real_rows, imag_rows = link_parts
    real_out = []
    imag_out = []
    for target in range(3):
        real_sum = 0.0
        imag_sum = 0.0
        for source in range(3):
            if dagger:
                coef_real = real_rows[source][target]
                coef_imag = -imag_rows[source][target]
            else:
                coef_real = real_rows[target][source]
                coef_imag = imag_rows[target][source]
            real_sum = real_sum + coef_real * real_vec[source] - coef_imag * imag_vec[source]
            imag_sum = imag_sum + coef_real * imag_vec[source] + coef_imag * real_vec[source]
        real_out.append(real_sum)
        imag_out.append(imag_sum)
    return (real_out, imag_out)

def spinor_hop(spinor, link_parts, dagger, direction, sign_value):
    real_vec = [spinor[:, :, 0, colour] for colour in range(3)]
    imag_vec = [spinor[:, :, 1, colour] for colour in range(3)]
    real_out, imag_out = colour_apply(link_parts, real_vec, imag_vec, dagger)
    turned = jnp.stack([jnp.stack(real_out, axis=2), jnp.stack(imag_out, axis=2)], axis=2)
    return turned + sign_value * gamma_apply(turned, direction)

def apply_hops(spinor, gauge_links, back_links, ahead_list, behind):
    hop_sum = jnp.zeros_like(spinor)
    for direction in range(4):
        hop_sum = hop_sum + spinor_hop(ahead_list[direction], link_lists(gauge_links[direction]), False, direction, -1.0)
        hop_sum = hop_sum + spinor_hop(behind[direction], link_lists(back_links[direction]), True, direction, 1.0)
    return spinor - HOPPING * hop_sum

def covariant_gradients(center, ahead_z, behind_z, gauge_links, back_z):
    ahead_list = [along_x(center, 1, SX), along_y(center, 1, SX), ahead_z]
    behind = [along_x(center, -1, SX), along_y(center, -1, SX), behind_z]
    back_links = [along_x(gauge_links[0], -1, SX), along_y(gauge_links[1], -1, SX), back_z]
    results = []
    for direction in range(3):
        forward_vec = ahead_list[direction]
        backward_vec = behind[direction]
        fore_real, fore_imag = colour_apply(link_lists(gauge_links[direction]), [forward_vec[..., colour, :, :] for colour in range(3)], [forward_vec[..., 3 + colour, :, :] for colour in range(3)], False)
        back_real, back_imag = colour_apply(link_lists(back_links[direction]), [backward_vec[..., colour, :, :] for colour in range(3)], [backward_vec[..., 3 + colour, :, :] for colour in range(3)], True)
        parts_out = [0.5 * (fore_real[colour] - back_real[colour]) for colour in range(3)]
        parts_out = parts_out + [0.5 * (fore_imag[colour] - back_imag[colour]) for colour in range(3)]
        results.append(jnp.stack(parts_out, axis=-3).astype(jnp.bfloat16))
    return jnp.stack(results, axis=-5)

def wilson_global(spinor, gauge_links):
    count_t = spinor.shape[4]
    slice_index = jnp.arange(count_t)
    edge_up = jnp.where(slice_index == count_t - 1, -1.0, 1.0)[:, None, None]
    edge_down = jnp.where(slice_index == 0, -1.0, 1.0)[:, None, None]
    ahead_list = [along_x(spinor, 1, SX), along_y(spinor, 1, SX), jnp.roll(spinor, -1, axis=5), jnp.roll(spinor, -1, axis=4) * edge_up]
    behind = [along_x(spinor, -1, SX), along_y(spinor, -1, SX), jnp.roll(spinor, 1, axis=5), jnp.roll(spinor, 1, axis=4) * edge_down]
    back_links = [along_x(gauge_links[0], -1, SX), along_y(gauge_links[1], -1, SX), jnp.roll(gauge_links[2], 1, axis=2), jnp.roll(gauge_links[3], 1, axis=1)]
    return apply_hops(spinor, gauge_links, back_links, ahead_list, behind)

def reference(right_sides, gauge_links, eigenvectors, step_lengths):
    count_r = right_sides.shape[0]
    spinor_shape = (count_r, 4, 2, 3) + right_sides.shape[2:]
    residual = right_sides.reshape(spinor_shape)
    solution = jnp.zeros_like(residual)
    for iteration in range(ITERS):
        solution = solution + step_lengths[iteration] * residual
        if iteration + 1 < ITERS:
            residual = residual - step_lengths[iteration] * wilson_global(residual, gauge_links)
    solution_flat = solution.reshape(right_sides.shape)
    rounded = solution_flat.astype(jnp.bfloat16)
    site_scale = 1.0 / math.sqrt(eigenvectors.shape[3] * eigenvectors.shape[4])
    count_k = eigenvectors.shape[1]
    slice_links = jnp.moveaxis(gauge_links, 2, 0)
    slice_solution = jnp.moveaxis(rounded, 2, 0)

    def one_slice(inputs):
        vectors, link_slice, solution_slice = inputs
        gradients = covariant_gradients(vectors, jnp.roll(vectors, -1, axis=2), jnp.roll(vectors, 1, axis=2), link_slice, jnp.roll(link_slice[2], 1, axis=1))
        flipped = jnp.concatenate([-vectors[:, 3:], vectors[:, :3]], axis=1)
        stacked = jnp.stack([vectors, flipped]).reshape(2, count_k, -1).astype(jnp.float32)
        grads_flat = gradients.reshape(3, count_k, -1).astype(jnp.float32)
        correlation = jnp.einsum('pkc,dlc->kdpl', stacked, grads_flat) * site_scale
        spinors = solution_slice.reshape(count_r, 4, -1).astype(jnp.float32)
        projection = jnp.einsum('pkc,rsc->krps', stacked, spinors) * site_scale
        return (correlation, projection.reshape(count_k, count_r, 8))
    correlations, perambulator = lax.map(one_slice, (eigenvectors, slice_links, slice_solution))
    return (solution_flat, correlations, perambulator)
```

```python
import functools
import math

import jax
import jax.numpy as jnp
from jax import lax
from jax.experimental import pallas as pl
from jax.experimental.pallas import tpu as pltpu
from jax.sharding import PartitionSpec as P

MESH = pl.DeviceIdType.MESH
F32 = jnp.float32
BF16 = jnp.bfloat16
SX = 16
ITERS = 4
HOPPING = 0.1
GAMMA_TABLE = (
    ((3, 0, 1), (2, 0, 1), (1, 0, -1), (0, 0, -1)),
    ((3, -1, 0), (2, 1, 0), (1, 1, 0), (0, -1, 0)),
    ((2, 0, 1), (3, 0, -1), (0, 0, -1), (1, 0, 1)),
    ((2, 1, 0), (3, 1, 0), (0, 1, 0), (1, 1, 0)),
)


def dot_nt(a, b):
    return lax.dot_general(a, b, (((1,), (1,)), ((), ())), preferred_element_type=F32)


def plus(a, b, sign):
    return a + b if sign > 0 else a - b


def phased(re, im, pr, pi):
    if pi == 0:
        return (pr, re), (pr, im)
    return (-pi, im), (pi, re)


def project(psi, direction, sign):
    re, im = [], []
    for target in range(2):
        source, pr, pi = GAMMA_TABLE[direction][target]
        (s0, a0), (s1, a1) = phased(psi[source][0], psi[source][1], pr, pi)
        re.append(plus(psi[target][0], a0, sign * s0))
        im.append(plus(psi[target][1], a1, sign * s1))
    return jnp.stack(re), jnp.stack(im)


def rebuild(acc, re, im, direction, sign):
    for target in range(4):
        if target < 2:
            terms = ((1, re[target]), (1, im[target]))
        else:
            source, pr, pi = GAMMA_TABLE[direction][target]
            (s0, a0), (s1, a1) = phased(re[source], im[source], pr, pi)
            terms = ((sign * s0, a0), (sign * s1, a1))
        for part in range(2):
            s, a = terms[part]
            old = acc[target][part]
            if old is None:
                acc[target][part] = a if s > 0 else -a
            else:
                acc[target][part] = plus(old, a, s)


def colour(u, re, im, dagger):
    out_re = out_im = None
    for b in range(3):
        ur = u[0, b] if dagger else u[0, :, b]
        ui = u[1, b] if dagger else u[1, :, b]
        vr, vi = re[:, b][:, None], im[:, b][:, None]
        ur, ui = ur[None], ui[None]
        t0 = plus(ur * vr, ui * vi, 1 if dagger else -1)
        t1 = plus(ur * vi, ui * vr, -1 if dagger else 1)
        out_re = t0 if out_re is None else out_re + t0
        out_im = t1 if out_im is None else out_im + t1
    return out_re, out_im


def roll(v, shift, axis):
    shape = v.shape
    flat = v.reshape((-1,) + shape[-2:])
    return pltpu.roll(flat, shift % shape[axis - 2 + len(shape)], axis=1 + axis).reshape(shape)


def kernel(
    sizes, al_ref, rs_ref, u8_ref, lz_ref, v_ref,
    sol_ref, cor_ref, per_ref,
    res, total, hsum, tsend, trecv, zsend, zrecv, w_ref, ub_ref, perm, g_ref, vo_ref, relay, s_ref,
    csend, crecv, psend, precv,
    t_ss, t_rs, z_ss, z_rs, vh_ss, vh_rs, uh_ss, uh_rs, loc_s,
    o_ss, o_rs, r_ss, r_rs, c_ss, c_rs, p_ss, p_rs,
):
    n_grp, n_ta, n_xyz, scale = sizes
    grp = lax.axis_index("grp")
    ta = lax.axis_index("ta")
    me = lax.axis_index("xyz")
    half_ta = n_ta // 2
    y = grp * 2 + ta // half_ta
    x = ta % half_ta

    def y_device(step):
        other = (y + step + 4) % 4
        return (other // 2, (other % 2) * half_ta + x, me)

    y_up, y_down = y_device(1), y_device(-1)
    z_next = (grp, ta, (me + 1) % n_xyz)
    z_prev = (grp, ta, (me + n_xyz - 1) % n_xyz)
    t_next = (grp, (ta + 1) % n_ta, me)
    t_prev = (grp, (ta + n_ta - 1) % n_ta, me)

    barrier = pltpu.get_barrier_semaphore()
    for device in (y_up, y_down, t_next, t_prev):
        pl.semaphore_signal(barrier, inc=1, device_id=device, device_id_type=MESH)

    @pl.loop(1, n_xyz)
    def _(o):
        pl.semaphore_signal(
            barrier, inc=1, device_id=(grp, ta, (me + o) % n_xyz), device_id_type=MESH
        )

    def remote(src, dst, ss, rs, device):
        return pltpu.make_async_remote_copy(
            src_ref=src, dst_ref=dst, send_sem=ss, recv_sem=rs, device_id=device,
            device_id_type=MESH,
        )

    lane = lax.broadcasted_iota(jnp.int32, (8, 128), 1)
    sub = lax.broadcasted_iota(jnp.int32, (8, 128), 0)
    column = lane % SX
    z_is0 = sub % 2 == 0

    def shift_x(v, step):
        if step > 0:
            return jnp.where(column == SX - 1, roll(v, SX - 1, 1), roll(v, -1, 1))
        return jnp.where(column == 0, roll(v, 1 - SX, 1), roll(v, 1, 1))

    def shift_y(v, step):
        a = roll(v, -step * SX, 1)
        keep = lane < 128 - SX if step > 0 else lane >= SX
        return jnp.where(keep, a, roll(a, 4, 0))

    def spins(ref):
        v = ref[...]
        return [[v[6 * s + 3 * p : 6 * s + 3 * p + 3] for p in range(2)] for s in range(4)]

    t_copies = lambda n: (
        remote(tsend.at[n, 0], trecv.at[n, 0], t_ss.at[n, 0], t_rs.at[n, 0], t_prev),
        remote(tsend.at[n, 1], trecv.at[n, 1], t_ss.at[n, 1], t_rs.at[n, 1], t_next),
        remote(zsend.at[n, 0], zrecv.at[n, 0], z_ss.at[n, 0], z_rs.at[n, 0], z_prev),
        remote(zsend.at[n, 1], zrecv.at[n, 1], z_ss.at[n, 1], z_rs.at[n, 1], z_next),
    )

    def prepare(n):
        psi = spins(res)
        re, im = project(psi, 3, -1)
        tsend[n, 0, 0], tsend[n, 0, 1] = re, im
        re, im = colour(u8_ref[3], *project(psi, 3, 1), True)
        tsend[n, 1, 0], tsend[n, 1, 1] = re, im
        re, im = project(psi, 2, -1)
        zsend[n, 0, 0] = jnp.where(z_is0, re[0], roll(re[1], 1, 0))
        zsend[n, 0, 1] = jnp.where(z_is0, im[0], roll(im[1], 1, 0))
        re, im = colour(u8_ref[2], *project(psi, 2, 1), True)
        zsend[n, 1, 0] = jnp.where(z_is0, roll(re[1], 7, 0), re[0])
        zsend[n, 1, 1] = jnp.where(z_is0, roll(im[1], 7, 0), im[0])

    def local_hops():
        psi = spins(res)
        acc = [[None, None] for _ in range(4)]
        for d, shift in ((0, shift_x), (1, shift_y)):
            re, im = project(psi, d, -1)
            rebuild(acc, *colour(u8_ref[d], shift(re, 1), shift(im, 1), False), d, -1)
            re, im = colour(u8_ref[d], *project(psi, d, 1), True)
            rebuild(acc, shift(re, -1), shift(im, -1), d, 1)
        for s in range(4):
            for p in range(2):
                k = 6 * s + 3 * p
                hsum[k : k + 3] = acc[s][p]

    def finish(n):
        psi = spins(res)
        acc = spins(hsum)
        sign_up = jnp.where(ta == n_ta - 1, -1.0, 1.0).astype(F32)
        sign_down = jnp.where(ta == 0, -1.0, 1.0).astype(F32)
        re, im = project(psi, 2, -1)

        def ahead(v, got):
            return jnp.where(z_is0, roll(v, 7, 0), jnp.stack([roll(got, 1, 0), got]))

        re, im = ahead(re, zrecv[n, 0, 0]), ahead(im, zrecv[n, 0, 1])
        rebuild(acc, *colour(u8_ref[2], re, im, False), 2, -1)
        re, im = colour(u8_ref[2], *project(psi, 2, 1), True)

        def behind(v, got):
            return jnp.where(z_is0, jnp.stack([roll(got, 7, 0), got]), roll(v, 1, 0))

        re, im = behind(re, zrecv[n, 1, 0]), behind(im, zrecv[n, 1, 1])
        rebuild(acc, re, im, 2, 1)
        re, im = trecv[n, 0, 0] * sign_up, trecv[n, 0, 1] * sign_up
        rebuild(acc, *colour(u8_ref[3], re, im, False), 3, -1)
        rebuild(acc, trecv[n, 1, 0] * sign_down, trecv[n, 1, 1] * sign_down, 3, 1)
        step = al_ref[n]
        step_after = al_ref[n + 1]
        for s in range(4):
            for p in range(2):
                k = 6 * s + 3 * p
                old = psi[s][p]
                new = old - step * (old - HOPPING * acc[s][p])
                res[k : k + 3] = new
                total[k : k + 3] = total[k : k + 3] + step_after * new

    res[...] = rs_ref[...]
    total[...] = al_ref[0] * rs_ref[...]
    prepare(0)

    pl.semaphore_wait(barrier, n_xyz - 1 + 4)
    for copy in t_copies(0):
        copy.start()
    halo_copies = (
        remote(v_ref.at[:, pl.ds(0, 1536)], w_ref.at[1, 4], vh_ss.at[0], vh_rs.at[0], z_prev),
        remote(v_ref.at[:, pl.ds(1536, 1536)], w_ref.at[0, 5], vh_ss.at[1], vh_rs.at[1], z_next),
        remote(lz_ref.at[1, 2], ub_ref.at[0, 2], uh_ss, uh_rs, z_next),
    )
    for copy in halo_copies:
        copy.start()

    def own_copy(c, direction):
        piece = pl.ds(c * 512, 512)
        return remote(
            v_ref.at[:, piece], relay.at[c], o_ss.at[c], o_rs.at[c],
            y_up if direction == 0 else y_down,
        )

    def relay_copy(c, direction):
        piece = pl.ds(c * 512, 512)
        return remote(
            relay.at[c], vo_ref.at[:, piece], r_ss.at[c], r_rs.at[c],
            y_up if direction == 0 else y_down,
        )

    for c in range(3):
        own_copy(c, 0).start()
        own_copy(c + 3, 1).start()
    local_copies = (
        pltpu.make_async_copy(v_ref.at[:, pl.ds(1536, 1536)], w_ref.at[0, 4], loc_s.at[0]),
        pltpu.make_async_copy(v_ref.at[:, pl.ds(0, 1536)], w_ref.at[1, 5], loc_s.at[1]),
        pltpu.make_async_copy(lz_ref.at[0, 2], ub_ref.at[1, 2], loc_s.at[2]),
    )
    for copy in local_copies:
        copy.start()

    src = lax.broadcasted_iota(jnp.int32, (256, 256), 0)
    dst = lax.broadcasted_iota(jnp.int32, (256, 256), 1)
    dcol = dst % SX
    froms = (
        jnp.where(dcol == SX - 1, dst - (SX - 1), dst + 1),
        jnp.where(dcol == 0, dst + (SX - 1), dst - 1),
        jnp.where(dst >= 256 - SX, dst - (256 - SX), dst + SX),
        jnp.where(dst < SX, dst + (256 - SX), dst - SX),
    )
    for k in range(4):
        perm[:, 256 * k : 256 * (k + 1)] = jnp.where(src == froms[k], 1.0, 0.0).astype(BF16)

    lcol = lax.broadcasted_iota(jnp.int32, (18, 256), 1) % SX
    for z in range(2):
        links = lz_ref[z, 0]
        ub_ref[z, 0] = jnp.where(
            lcol == 0, pltpu.roll(links, 256 - (SX - 1), axis=1), pltpu.roll(links, 1, axis=1)
        )
        ub_ref[z, 1] = pltpu.roll(lz_ref[z, 1], SX, axis=1)

    @pl.loop(0, 12)
    def _(i):
        z, m = i // 6, i % 6
        block = v_ref[:, pl.ds(pl.multiple_of(i * 256, 256), 256)]
        out = jnp.dot(block, perm[...], preferred_element_type=F32).astype(BF16)
        for k in range(4):
            w_ref[z, k, :, pl.ds(pl.multiple_of(m * 256, 256), 256)] = out[
                :, 256 * k : 256 * (k + 1)
            ]

    def gradient(d):
        @pl.loop(0, 4)
        def _(q):
            z, h = q // 2, q % 2
            lanes = pl.ds(pl.multiple_of(h * 128, 128), 128)

            def part(m):
                return pl.ds(pl.multiple_of(m * 256 + h * 128, 128), 128)

            @pl.loop(0, 8)
            def _(kc):
                rows = pl.ds(pl.multiple_of(kc * 16, 16), 16)
                outs = []
                for side in range(2):
                    v = [w_ref[z, 2 * d + side, rows, part(m)].astype(F32) for m in range(6)]
                    l_ref = lz_ref if side == 0 else ub_ref
                    u = [
                        jnp.broadcast_to(l_ref[z, d, i : i + 1, lanes], (16, 128))
                        for i in range(18)
                    ]
                    for a in range(3):
                        re = im = None
                        for b in range(3):
                            if side == 0:
                                ur, ui = u[3 * a + b], u[9 + 3 * a + b]
                                t0 = ur * v[b] - ui * v[3 + b]
                                t1 = ur * v[3 + b] + ui * v[b]
                            else:
                                ur, ui = u[3 * b + a], u[9 + 3 * b + a]
                                t0 = ur * v[b] + ui * v[3 + b]
                                t1 = ur * v[3 + b] - ui * v[b]
                            re = t0 if re is None else re + t0
                            im = t1 if im is None else im + t1
                        outs.append((re, im))
                for a in range(3):
                    re = (0.5 * (outs[a][0] - outs[3 + a][0])).astype(BF16)
                    im = (0.5 * (outs[a][1] - outs[3 + a][1])).astype(BF16)
                    below = pl.ds(pl.multiple_of(128 + kc * 16, 16), 16)
                    g_ref[d, rows, part(z * 6 + a)] = re
                    g_ref[d, rows, part(z * 6 + 3 + a)] = im
                    g_ref[d, below, part(z * 6 + a)] = im
                    g_ref[d, below, part(z * 6 + 3 + a)] = -re

    s_ref[...] = jnp.zeros_like(s_ref)
    for n in range(ITERS - 1):
        if n > 0:
            prepare(n)
            for copy in t_copies(n):
                copy.start()
        local_hops()
        if n == 2:
            for copy in halo_copies:
                copy.wait()
            for copy in local_copies:
                copy.wait()
        gradient(n)
        for direction in range(2):
            c = n + 3 * direction
            own_copy(c, direction).wait()
            relay_copy(c, direction).start()
        for copy in t_copies(n):
            copy.wait()
        finish(n)

    sol_ref[...] = total[...]

    row = lax.broadcasted_iota(jnp.int32, (96, 48), 0)
    col = lax.broadcasted_iota(jnp.int32, (96, 48), 1)
    row_m, row_r, row_p, row_s = row // 16, (row // 8) % 2, (row // 4) % 2, row % 4
    col_r, col_s, col_m = col // 24, (col // 6) % 4, col % 6
    same = (row_r == col_r) & (row_s == col_s)
    want = jnp.where(row_p == 0, row_m, (row_m + 3) % 6)
    value = jnp.where((row_p == 1) & (row_m >= 3), -1.0, 1.0)
    pick = jnp.where(same & (want == col_m), value, 0.0).astype(BF16)
    flat = total[...]
    for z in range(2):
        rows = []
        for r in range(2):
            halves = [flat[:, 4 * h + 2 * r + z, :] for h in range(2)]
            rows.append(jnp.concatenate(halves, axis=1))
        spinors = jnp.concatenate(rows, axis=0).astype(BF16)
        placed = jnp.dot(pick, spinors, preferred_element_type=F32).astype(BF16)
        for m in range(6):
            s_ref[0:16, (z * 6 + m) * 256 : (z * 6 + m + 1) * 256] = placed[16 * m : 16 * m + 16]

    def c_copy(target, o):
        return remote(
            csend.at[target], crecv.at[o], c_ss.at[o], c_rs.at[o], (grp, ta, target)
        )

    def p_copy(target, o):
        return remote(
            psend.at[target], precv.at[o], p_ss.at[o], p_rs.at[o], (grp, ta, target)
        )

    lane3 = lax.broadcasted_iota(jnp.int32, (8, 8, 128), 2)

    def products(vectors_ref, first):
        for d in range(3):
            c = dot_nt(vectors_ref[...], g_ref[d]).astype(BF16)
            csend[pl.ds(first, 8), :, 256 * d : 256 * (d + 1)] = c.reshape(8, 16, 256)
        p = dot_nt(vectors_ref[...], s_ref[...]).reshape(8, 2, 8, 128)
        psend[pl.ds(first, 8)] = jnp.where(lane3 < 16, p[:, 0], pltpu.roll(p[:, 1], 16, axis=2))

        @pl.loop(0, 8)
        def _(i):
            target = first + i
            o = (target - me + n_xyz) % n_xyz

            @pl.when(o != 0)
            def _():
                c_copy(target, o).start()
                p_copy(target, o).start()

    products(v_ref, grp * 8)
    for direction in range(2):
        for c in range(3):
            relay_copy(c + 3 * direction, direction).wait()
    products(vo_ref, (1 - grp) * 8)

    @pl.loop(1, n_xyz)
    def _(o):
        target = (me + o) % n_xyz
        c_copy(target, o).wait()
        p_copy(target, o).wait()

    c_sum = csend[me].astype(F32)
    p_sum = psend[me]
    for o in range(1, n_xyz):
        c_sum = c_sum + crecv[o].astype(F32)
        p_sum = p_sum + precv[o]
    cor_ref[...] = c_sum * scale
    p_sum = p_sum * scale
    tall = jnp.concatenate([p_sum, pltpu.roll(p_sum, 112, axis=1)], axis=0)
    wide = jnp.concatenate([tall, jnp.zeros((112, 128), F32)], axis=0).T
    per_ref[0] = wide[0:8]
    per_ref[1] = wide[8:16]


def body(sizes, right_sides, gauge_links, eigenvectors, step_lengths):
    rs = right_sides.reshape(2, 24, 2, 2, 128)
    rs = rs.transpose(1, 3, 0, 2, 4).reshape(24, 8, 128)
    links = gauge_links.reshape(4, 18, 2, 256)
    lz = links.transpose(2, 0, 1, 3)
    u8 = links.reshape(72, 2, 2, 128).transpose(0, 2, 1, 3)[:, :, None]
    u8 = jnp.broadcast_to(u8, (72, 2, 2, 2, 128)).reshape(4, 2, 3, 3, 8, 128)
    v = eigenvectors.reshape(128, 6, 2, 256).transpose(0, 2, 1, 3).reshape(128, 3072)
    vmem = pl.BlockSpec(memory_space=pltpu.VMEM)
    n_it = ITERS - 1
    dma = pltpu.SemaphoreType.DMA
    sol, cor, per = pl.pallas_call(
        functools.partial(kernel, sizes),
        out_shape=(
            jax.ShapeDtypeStruct((24, 8, 128), F32),
            jax.ShapeDtypeStruct((16, 768), F32),
            jax.ShapeDtypeStruct((2, 8, 128), F32),
        ),
        in_specs=[pl.BlockSpec(memory_space=pltpu.SMEM), vmem, vmem, vmem, vmem],
        out_specs=(vmem, vmem, vmem),
        scratch_shapes=[
            pltpu.VMEM((24, 8, 128), F32),
            pltpu.VMEM((24, 8, 128), F32),
            pltpu.VMEM((24, 8, 128), F32),
            pltpu.VMEM((n_it, 2, 2, 2, 3, 8, 128), F32),
            pltpu.VMEM((n_it, 2, 2, 2, 3, 8, 128), F32),
            pltpu.VMEM((n_it, 2, 2, 3, 8, 128), F32),
            pltpu.VMEM((n_it, 2, 2, 3, 8, 128), F32),
            pltpu.VMEM((2, 6, 128, 1536), BF16),
            pltpu.VMEM((2, 3, 18, 256), F32),
            pltpu.VMEM((256, 1024), BF16),
            pltpu.VMEM((3, 256, 3072), BF16),
            pltpu.VMEM((128, 3072), BF16),
            pltpu.VMEM((6, 128, 512), BF16),
            pltpu.VMEM((128, 3072), BF16),
            pltpu.VMEM((16, 16, 768), BF16),
            pltpu.VMEM((16, 16, 768), BF16),
            pltpu.VMEM((16, 8, 128), F32),
            pltpu.VMEM((16, 8, 128), F32),
            dma((n_it, 2)), dma((n_it, 2)), dma((n_it, 2)), dma((n_it, 2)),
            dma((2,)), dma((2,)), dma(()), dma(()), dma((3,)),
            dma((6,)), dma((6,)), dma((6,)), dma((6,)),
            dma((16,)), dma((16,)), dma((16,)), dma((16,)),
        ],
        compiler_params=pltpu.CompilerParams(
            collective_id=0, has_side_effects=True, vmem_limit_bytes=56 * 1024 * 1024
        ),
    )(step_lengths, rs, u8, lz, v)
    sol = sol.reshape(24, 2, 2, 2, 128).transpose(2, 0, 3, 1, 4).reshape(right_sides.shape)
    cor = cor.reshape(1, 16, 3, 2, 128)
    per = per[:, :, :16].transpose(2, 0, 1)[None]
    return sol, cor, per


def solution(mesh):
    n_grp, n_ta, n_xyz = (mesh.shape[a] for a in ("grp", "ta", "xyz"))
    scale = 1.0 / math.sqrt(2 * n_xyz * 256)
    return jax.shard_map(
        functools.partial(body, (n_grp, n_ta, n_xyz, scale)),
        mesh=mesh,
        in_specs=(
            P("grp", None, "ta", "xyz", None),
            P(None, None, "ta", "xyz", None),
            P("ta", "grp", None, "xyz", None),
            P(),
        ),
        out_specs=(
            P("grp", None, "ta", "xyz", None),
            P("ta", "xyz", None, None, "grp"),
            P("ta", "xyz", "grp", None),
        ),
        check_vma=False,
    )
```

```python
import functools
import math

import jax
import jax.numpy as jnp
from jax import lax
from jax.experimental import pallas as pl
from jax.experimental.pallas import tpu as pltpu
from jax.sharding import PartitionSpec as P

MESH = pl.DeviceIdType.MESH
F32 = jnp.float32
BF16 = jnp.bfloat16
SX = 16
ITERS = 4
HOPPING = 0.1
GAMMA_TABLE = (
    ((3, 0, 1), (2, 0, 1), (1, 0, -1), (0, 0, -1)),
    ((3, -1, 0), (2, 1, 0), (1, 1, 0), (0, -1, 0)),
    ((2, 0, 1), (3, 0, -1), (0, 0, -1), (1, 0, 1)),
    ((2, 1, 0), (3, 1, 0), (0, 1, 0), (1, 1, 0)),
)


def dot_nt(a, b):
    return lax.dot_general(a, b, (((1,), (1,)), ((), ())), preferred_element_type=F32)


def plus(a, b, sign):
    return a + b if sign > 0 else a - b


def phased(re, im, pr, pi):
    if pi == 0:
        return (pr, re), (pr, im)
    return (-pi, im), (pi, re)


def project(psi, direction, sign):
    re, im = [], []
    for target in range(2):
        source, pr, pi = GAMMA_TABLE[direction][target]
        (s0, a0), (s1, a1) = phased(psi[source][0], psi[source][1], pr, pi)
        re.append(plus(psi[target][0], a0, sign * s0))
        im.append(plus(psi[target][1], a1, sign * s1))
    return jnp.stack(re), jnp.stack(im)


def rebuild(acc, re, im, direction, sign):
    for target in range(4):
        if target < 2:
            terms = ((1, re[target]), (1, im[target]))
        else:
            source, pr, pi = GAMMA_TABLE[direction][target]
            (s0, a0), (s1, a1) = phased(re[source], im[source], pr, pi)
            terms = ((sign * s0, a0), (sign * s1, a1))
        for part in range(2):
            s, a = terms[part]
            old = acc[target][part]
            if old is None:
                acc[target][part] = a if s > 0 else -a
            else:
                acc[target][part] = plus(old, a, s)


def colour(u, re, im, dagger):
    out_re = out_im = None
    for b in range(3):
        ur = u[0, b] if dagger else u[0, :, b]
        ui = u[1, b] if dagger else u[1, :, b]
        vr, vi = re[:, b][:, None], im[:, b][:, None]
        ur, ui = ur[None], ui[None]
        t0 = plus(ur * vr, ui * vi, 1 if dagger else -1)
        t1 = plus(ur * vi, ui * vr, -1 if dagger else 1)
        out_re = t0 if out_re is None else out_re + t0
        out_im = t1 if out_im is None else out_im + t1
    return out_re, out_im


def roll(v, shift, axis):
    shape = v.shape
    flat = v.reshape((-1,) + shape[-2:])
    return pltpu.roll(flat, shift % shape[axis - 2 + len(shape)], axis=1 + axis).reshape(shape)


def kernel(
    sizes, al_ref, rs_hbm, lk_hbm, v_hbm,
    sol_ref, cor_ref, per_ref,
    rs_v, lk_v, vraw, v32, vall, relay, u8, lz, uz,
    res, total, hsum, tsend, trecv, zsend, zrecv, w_ref, ub_ref, perm, g_ref, s_ref,
    csend, crecv, psend, precv,
    t_ss, t_rs, z_ss, z_rs, vh_ss, vh_rs, uh_ss, uh_rs, loc_s,
    o_ss, o_rs, r_ss, r_rs, c_ss, c_rs, p_ss, p_rs,
):
    n_grp, n_ta, n_xyz, scale = sizes
    grp = lax.axis_index("grp")
    ta = lax.axis_index("ta")
    me = lax.axis_index("xyz")
    half_ta = n_ta // 2
    y = grp * 2 + ta // half_ta
    x = ta % half_ta

    def y_device(step):
        other = (y + step + 4) % 4
        return (other // 2, (other % 2) * half_ta + x, me)

    z_next = (grp, ta, (me + 1) % n_xyz)
    z_prev = (grp, ta, (me + n_xyz - 1) % n_xyz)
    t_next = (grp, (ta + 1) % n_ta, me)
    t_prev = (grp, (ta + n_ta - 1) % n_ta, me)

    barrier = pltpu.get_barrier_semaphore()
    for device in (y_device(1), y_device(-1), t_next, t_prev):
        pl.semaphore_signal(barrier, inc=1, device_id=device, device_id_type=MESH)

    @pl.loop(1, n_xyz)
    def _(o):
        pl.semaphore_signal(
            barrier, inc=1, device_id=(grp, ta, (me + o) % n_xyz), device_id_type=MESH
        )

    fetches = (
        pltpu.make_async_copy(lk_hbm, lk_v, loc_s.at[0]),
        pltpu.make_async_copy(rs_hbm, rs_v, loc_s.at[1]),
        pltpu.make_async_copy(v_hbm, vraw.at[0], loc_s.at[2]),
    )
    for copy in fetches:
        copy.start()

    def remote(src, dst, ss, rs, device):
        return pltpu.make_async_remote_copy(
            src_ref=src, dst_ref=dst, send_sem=ss, recv_sem=rs, device_id=device,
            device_id_type=MESH,
        )

    lane = lax.broadcasted_iota(jnp.int32, (8, 128), 1)
    sub = lax.broadcasted_iota(jnp.int32, (8, 128), 0)
    column = lane % SX
    z_is0 = sub % 2 == 0

    def shift_x(v, step):
        if step > 0:
            return jnp.where(column == SX - 1, roll(v, SX - 1, 1), roll(v, -1, 1))
        return jnp.where(column == 0, roll(v, 1 - SX, 1), roll(v, 1, 1))

    def shift_y(v, step):
        a = roll(v, -step * SX, 1)
        keep = lane < 128 - SX if step > 0 else lane >= SX
        return jnp.where(keep, a, roll(a, 4, 0))

    def spins(ref):
        v = ref[...].reshape(24, 8, 128)
        return [[v[6 * s + 3 * p : 6 * s + 3 * p + 3] for p in range(2)] for s in range(4)]

    def put(ref, s, p, value):
        k = 8 * (6 * s + 3 * p)
        ref[k : k + 24, :] = value.reshape(24, 128)

    def links_of(d):
        return u8[144 * d : 144 * (d + 1), :].reshape(2, 3, 3, 8, 128)

    def t_copies(n):
        return (
            remote(tsend.at[n, 0], trecv.at[n, 0], t_ss.at[n, 0], t_rs.at[n, 0], t_prev),
            remote(tsend.at[n, 1], trecv.at[n, 1], t_ss.at[n, 1], t_rs.at[n, 1], t_next),
            remote(zsend.at[n, 0], zrecv.at[n, 0], z_ss.at[n, 0], z_rs.at[n, 0], z_prev),
            remote(zsend.at[n, 1], zrecv.at[n, 1], z_ss.at[n, 1], z_rs.at[n, 1], z_next),
        )

    def prepare(n):
        psi = spins(res)
        re, im = project(psi, 3, -1)
        tsend[n, 0, 0], tsend[n, 0, 1] = re, im
        re, im = colour(links_of(3), *project(psi, 3, 1), True)
        tsend[n, 1, 0], tsend[n, 1, 1] = re, im
        re, im = project(psi, 2, -1)
        zsend[n, 0, 0] = jnp.where(z_is0, re[0], roll(re[1], 1, 0))
        zsend[n, 0, 1] = jnp.where(z_is0, im[0], roll(im[1], 1, 0))
        re, im = colour(links_of(2), *project(psi, 2, 1), True)
        zsend[n, 1, 0] = jnp.where(z_is0, roll(re[1], 7, 0), re[0])
        zsend[n, 1, 1] = jnp.where(z_is0, roll(im[1], 7, 0), im[0])

    def local_hops():
        psi = spins(res)
        acc = [[None, None] for _ in range(4)]
        for d, shift in ((0, shift_x), (1, shift_y)):
            re, im = project(psi, d, -1)
            rebuild(acc, *colour(links_of(d), shift(re, 1), shift(im, 1), False), d, -1)
            re, im = colour(links_of(d), *project(psi, d, 1), True)
            rebuild(acc, shift(re, -1), shift(im, -1), d, 1)
        for s in range(4):
            for p in range(2):
                put(hsum, s, p, acc[s][p])

    def finish(n):
        psi = spins(res)
        acc = spins(hsum)
        sums = spins(total)
        sign_up = jnp.where(ta == n_ta - 1, -1.0, 1.0).astype(F32)
        sign_down = jnp.where(ta == 0, -1.0, 1.0).astype(F32)
        re, im = project(psi, 2, -1)

        def ahead(v, got):
            return jnp.where(z_is0, roll(v, 7, 0), jnp.stack([roll(got, 1, 0), got]))

        re, im = ahead(re, zrecv[n, 0, 0]), ahead(im, zrecv[n, 0, 1])
        rebuild(acc, *colour(links_of(2), re, im, False), 2, -1)
        re, im = colour(links_of(2), *project(psi, 2, 1), True)

        def behind(v, got):
            return jnp.where(z_is0, jnp.stack([roll(got, 7, 0), got]), roll(v, 1, 0))

        re, im = behind(re, zrecv[n, 1, 0]), behind(im, zrecv[n, 1, 1])
        rebuild(acc, re, im, 2, 1)
        re, im = trecv[n, 0, 0] * sign_up, trecv[n, 0, 1] * sign_up
        rebuild(acc, *colour(links_of(3), re, im, False), 3, -1)
        rebuild(acc, trecv[n, 1, 0] * sign_down, trecv[n, 1, 1] * sign_down, 3, 1)
        step = al_ref[n]
        step_after = al_ref[n + 1]
        for s in range(4):
            for p in range(2):
                old = psi[s][p]
                new = old - step * (old - HOPPING * acc[s][p])
                put(res, s, p, new)
                put(total, s, p, sums[s][p] + step_after * new)

    src = lax.broadcasted_iota(jnp.int32, (256, 256), 0)
    dst = lax.broadcasted_iota(jnp.int32, (256, 256), 1)
    dcol = dst % SX
    froms = (
        jnp.where(dcol == SX - 1, dst - (SX - 1), dst + 1),
        jnp.where(dcol == 0, dst + (SX - 1), dst - 1),
        jnp.where(dst >= 256 - SX, dst - (256 - SX), dst + SX),
        jnp.where(dst < SX, dst + (256 - SX), dst - SX),
    )
    for k in range(4):
        perm[:, 256 * k : 256 * (k + 1)] = jnp.where(src == froms[k], 1.0, 0.0).astype(BF16)
    s_ref[...] = jnp.zeros_like(s_ref)

    fetches[0].wait()
    fetches[1].wait()
    first_step = al_ref[0]
    for h in range(2):
        for z in range(2):
            links = lk_v[pl.ds(2 * h + z, 72, stride=4), :]
            for r in range(2):
                u8[pl.ds(4 * h + 2 * r + z, 72, stride=8), :] = links
                values = rs_v[pl.ds(96 * r + 2 * h + z, 24, stride=4), :]
                res[pl.ds(4 * h + 2 * r + z, 24, stride=8), :] = values
                total[pl.ds(4 * h + 2 * r + z, 24, stride=8), :] = first_step * values
            for d in range(3):
                rows = lk_v[pl.ds(72 * d + 2 * h + z, 18, stride=4), :]
                lz[z, d, :, 128 * h : 128 * (h + 1)] = rows
                if d == 2 and z == 1:
                    uz[:, 128 * h : 128 * (h + 1)] = rows
                if d == 2 and z == 0:
                    ub_ref[1, 2, :, 128 * h : 128 * (h + 1)] = rows
    lcol = lax.broadcasted_iota(jnp.int32, (18, 256), 1) % SX
    for z in range(2):
        links = lz[z, 0]
        ub_ref[z, 0] = jnp.where(
            lcol == 0, pltpu.roll(links, 256 - (SX - 1), axis=1), pltpu.roll(links, 1, axis=1)
        )
        ub_ref[z, 1] = pltpu.roll(lz[z, 1], SX, axis=1)

    pl.semaphore_wait(barrier, n_xyz - 1 + 4)

    def way(c):
        return y_device(1 - 2 * ((c // 2) % 2))

    def own_copy(c):
        rows = pl.ds(pl.multiple_of(c * 384, 384), 384)
        return remote(v_hbm.at[rows], relay.at[c], o_ss.at[c], o_rs.at[c], way(c))

    def relay_copy(c):
        rows = pl.ds(pl.multiple_of(c * 384, 384), 384)
        return remote(relay.at[c], vraw.at[1, rows], r_ss.at[c], r_rs.at[c], way(c))

    def pass_on(step):
        for c in (step + 2 * (step // 2), step + 2 * (step // 2) + 2):
            own_copy(c).wait()
            relay_copy(c).start()

    def sort_chunk(which, c):
        v32[...] = vraw[which, pl.ds(pl.multiple_of(c * 384, 384), 384), :].astype(F32)
        rows = pl.ds(pl.multiple_of(c * 16, 16), 16)
        for m in range(6):
            for h in range(2):
                for z in range(2):
                    k = (z * 6 + m) * 256 + h * 128
                    vall[which, rows, k : k + 128] = v32[
                        pl.ds(4 * m + 2 * h + z, 16, stride=24), :
                    ].astype(BF16)

    low, high = vall.at[0, :, pl.ds(0, 1536)], vall.at[0, :, pl.ds(1536, 1536)]
    halo_copies = (
        remote(low, w_ref.at[1, 4], vh_ss.at[0], vh_rs.at[0], z_prev),
        remote(high, w_ref.at[0, 5], vh_ss.at[1], vh_rs.at[1], z_next),
        remote(uz, ub_ref.at[0, 2], uh_ss, uh_rs, z_next),
        pltpu.make_async_copy(high, w_ref.at[0, 4], loc_s.at[0]),
        pltpu.make_async_copy(low, w_ref.at[1, 5], loc_s.at[1]),
    )

    def gradient(d):
        @pl.loop(0, 4)
        def _(q):
            z, h = q // 2, q % 2
            lanes = pl.ds(pl.multiple_of(h * 128, 128), 128)

            def part(m):
                return pl.ds(pl.multiple_of(m * 256 + h * 128, 128), 128)

            @pl.loop(0, 8)
            def _(kc):
                rows = pl.ds(pl.multiple_of(kc * 16, 16), 16)
                outs = []
                for side in range(2):
                    v = [w_ref[z, 2 * d + side, rows, part(m)].astype(F32) for m in range(6)]
                    l_ref = lz if side == 0 else ub_ref
                    u = [
                        jnp.broadcast_to(l_ref[z, d, i : i + 1, lanes], (16, 128))
                        for i in range(18)
                    ]
                    for a in range(3):
                        re = im = None
                        for b in range(3):
                            if side == 0:
                                ur, ui = u[3 * a + b], u[9 + 3 * a + b]
                                t0 = ur * v[b] - ui * v[3 + b]
                                t1 = ur * v[3 + b] + ui * v[b]
                            else:
                                ur, ui = u[3 * b + a], u[9 + 3 * b + a]
                                t0 = ur * v[b] + ui * v[3 + b]
                                t1 = ur * v[3 + b] - ui * v[b]
                            re = t0 if re is None else re + t0
                            im = t1 if im is None else im + t1
                        outs.append((re, im))
                for a in range(3):
                    re = (0.5 * (outs[a][0] - outs[3 + a][0])).astype(BF16)
                    im = (0.5 * (outs[a][1] - outs[3 + a][1])).astype(BF16)
                    above = pl.ds(pl.multiple_of(d * 256 + kc * 16, 16), 16)
                    below = pl.ds(pl.multiple_of(d * 256 + 128 + kc * 16, 16), 16)
                    g_ref[above, part(z * 6 + a)] = re
                    g_ref[above, part(z * 6 + 3 + a)] = im
                    g_ref[below, part(z * 6 + a)] = im
                    g_ref[below, part(z * 6 + 3 + a)] = -re

    @pl.loop(0, ITERS - 1)
    def _(n):
        prepare(n)
        for copy in t_copies(n):
            copy.start()

        @pl.when(n == 0)
        def _():
            @pl.loop(0, 8)
            def _(i):
                own_copy(i // 4 * 4 + (i % 2) * 2 + (i // 2) % 2).start()

        local_hops()

        @pl.when(n == 0)
        def _():
            fetches[2].wait()

            @pl.loop(0, 8)
            def _(c):
                sort_chunk(0, c)

            for copy in halo_copies:
                copy.start()

            @pl.loop(0, 12)
            def _(i):
                z, m = i // 6, i % 6
                block = vall[0, :, pl.ds(pl.multiple_of(i * 256, 256), 256)]
                out = jnp.dot(block, perm[...], preferred_element_type=F32).astype(BF16)
                for k in range(4):
                    w_ref[z, k, :, pl.ds(pl.multiple_of(m * 256, 256), 256)] = out[
                        :, 256 * k : 256 * (k + 1)
                    ]

        @pl.when(n == 2)
        def _():
            for copy in halo_copies:
                copy.wait()

        gradient(n)
        pass_on(n)
        for copy in t_copies(n):
            copy.wait()
        finish(n)

    pass_on(3)

    row = lax.broadcasted_iota(jnp.int32, (96, 48), 0)
    col = lax.broadcasted_iota(jnp.int32, (96, 48), 1)
    row_m, row_r, row_p, row_s = row // 16, (row // 8) % 2, (row // 4) % 2, row % 4
    col_r, col_s, col_m = col // 24, (col // 6) % 4, col % 6
    same = (row_r == col_r) & (row_s == col_s)
    want = jnp.where(row_p == 0, row_m, (row_m + 3) % 6)
    value = jnp.where((row_p == 1) & (row_m >= 3), -1.0, 1.0)
    pick = jnp.where(same & (want == col_m), value, 0.0).astype(BF16)
    for z in range(2):
        rows = []
        for r in range(2):
            halves = []
            for h in range(2):
                values = total[pl.ds(4 * h + 2 * r + z, 24, stride=8), :]
                sol_ref[pl.ds(96 * r + 2 * h + z, 24, stride=4), :] = values
                halves.append(values)
            rows.append(jnp.concatenate(halves, axis=1))
        spinors = jnp.concatenate(rows, axis=0).astype(BF16)
        placed = jnp.dot(pick, spinors, preferred_element_type=F32).astype(BF16)
        for m in range(6):
            s_ref[0:16, (z * 6 + m) * 256 : (z * 6 + m + 1) * 256] = placed[16 * m : 16 * m + 16]

    def c_copy(target, o):
        return remote(
            csend.at[target], crecv.at[o], c_ss.at[o], c_rs.at[o], (grp, ta, target)
        )

    def p_copy(target, o):
        return remote(
            psend.at[target], precv.at[o], p_ss.at[o], p_rs.at[o], (grp, ta, target)
        )

    lane3 = lax.broadcasted_iota(jnp.int32, (4, 8, 128), 2)

    @pl.loop(0, 4)
    def _(phase):
        which, half = phase // 2, phase % 2

        @pl.when(which == 1)
        def _():
            @pl.loop(0, 4)
            def _(j):
                relay_copy(4 * half + j).wait()
                sort_chunk(1, 4 * half + j)

        first = (grp + which - 2 * grp * which) * 8 + half * 4
        rows = pl.ds(pl.multiple_of(half * 64, 64), 64)

        @pl.loop(0, 3)
        def _(d):
            block = pl.ds(pl.multiple_of(d * 256, 256), 256)
            c = dot_nt(g_ref[block, :], vall[which, rows, :]).T.astype(BF16)
            csend[pl.ds(first, 4), :, block] = c.reshape(4, 16, 256)

        p = dot_nt(s_ref[...], vall[which, rows, :]).T.reshape(4, 2, 8, 128)
        psend[pl.ds(first, 4)] = jnp.where(lane3 < 16, p[:, 0], pltpu.roll(p[:, 1], 16, axis=2))

        @pl.loop(0, 4)
        def _(i):
            target = first + i
            o = (target - me + n_xyz) % n_xyz

            @pl.when(o != 0)
            def _():
                c_copy(target, o).start()
                p_copy(target, o).start()

    @pl.loop(1, n_xyz)
    def _(o):
        target = (me + o) % n_xyz
        c_copy(target, o).wait()
        p_copy(target, o).wait()

    c_sum = csend[me].astype(F32)
    p_sum = psend[me]
    for o in range(1, n_xyz):
        c_sum = c_sum + crecv[o].astype(F32)
        p_sum = p_sum + precv[o]
    for k in range(6):
        cor_ref[pl.ds(k, 16, stride=6), :] = c_sum[:, 128 * k : 128 * (k + 1)] * scale
    p_sum = p_sum * scale
    tall = jnp.concatenate([p_sum, pltpu.roll(p_sum, 112, axis=1)], axis=0)
    wide = jnp.concatenate([tall, jnp.zeros((112, 128), F32)], axis=0).T
    per_ref[0] = wide[0:8, 0:16]
    per_ref[1] = wide[8:16, 0:16]


def rows_of(array, lead):
    return array.reshape(lead, 2, 2, 128).transpose(0, 2, 1, 3).reshape(lead * 4, 128)


def body(sizes, right_sides, gauge_links, eigenvectors, step_lengths):
    vmem = pl.BlockSpec(memory_space=pltpu.VMEM)
    anywhere = pl.BlockSpec(memory_space=pl.ANY)
    n_it = ITERS - 1
    dma = pltpu.SemaphoreType.DMA
    sol, cor, per = pl.pallas_call(
        functools.partial(kernel, sizes),
        out_shape=(
            jax.ShapeDtypeStruct((192, 128), F32),
            jax.ShapeDtypeStruct((96, 128), F32),
            jax.ShapeDtypeStruct((2, 8, 16), F32),
        ),
        in_specs=[pl.BlockSpec(memory_space=pltpu.SMEM), anywhere, anywhere, anywhere],
        out_specs=(vmem, vmem, vmem),
        scratch_shapes=[
            pltpu.VMEM((192, 128), F32),
            pltpu.VMEM((288, 128), F32),
            pltpu.VMEM((2, 3072, 128), BF16),
            pltpu.VMEM((384, 128), F32),
            pltpu.VMEM((2, 128, 3072), BF16),
            pltpu.VMEM((8, 384, 128), BF16),
            pltpu.VMEM((576, 128), F32),
            pltpu.VMEM((2, 3, 18, 256), F32),
            pltpu.VMEM((18, 256), F32),
            pltpu.VMEM((192, 128), F32),
            pltpu.VMEM((192, 128), F32),
            pltpu.VMEM((192, 128), F32),
            pltpu.VMEM((n_it, 2, 2, 2, 3, 8, 128), F32),
            pltpu.VMEM((n_it, 2, 2, 2, 3, 8, 128), F32),
            pltpu.VMEM((n_it, 2, 2, 3, 8, 128), F32),
            pltpu.VMEM((n_it, 2, 2, 3, 8, 128), F32),
            pltpu.VMEM((2, 6, 128, 1536), BF16),
            pltpu.VMEM((2, 3, 18, 256), F32),
            pltpu.VMEM((256, 1024), BF16),
            pltpu.VMEM((768, 3072), BF16),
            pltpu.VMEM((128, 3072), BF16),
            pltpu.VMEM((16, 16, 768), BF16),
            pltpu.VMEM((16, 16, 768), BF16),
            pltpu.VMEM((16, 8, 128), F32),
            pltpu.VMEM((16, 8, 128), F32),
            dma((n_it, 2)), dma((n_it, 2)), dma((n_it, 2)), dma((n_it, 2)),
            dma((2,)), dma((2,)), dma(()), dma(()), dma((3,)),
            dma((8,)), dma((8,)), dma((8,)), dma((8,)),
            dma((16,)), dma((16,)), dma((16,)), dma((16,)),
        ],
        compiler_params=pltpu.CompilerParams(
            collective_id=0, has_side_effects=True, vmem_limit_bytes=56 * 1024 * 1024
        ),
    )(
        step_lengths,
        rows_of(right_sides, 48),
        rows_of(gauge_links, 72),
        rows_of(eigenvectors, 768),
    )
    sol = sol.reshape(48, 2, 2, 128).transpose(0, 2, 1, 3).reshape(right_sides.shape)
    cor = cor.reshape(1, 16, 3, 2, 128)
    return sol, cor, per.transpose(2, 0, 1)[None]


def solution(mesh):
    n_grp, n_ta, n_xyz = (mesh.shape[a] for a in ("grp", "ta", "xyz"))
    scale = 1.0 / math.sqrt(2 * n_xyz * 256)
    return jax.shard_map(
        functools.partial(body, (n_grp, n_ta, n_xyz, scale)),
        mesh=mesh,
        in_specs=(
            P("grp", None, "ta", "xyz", None),
            P(None, None, "ta", "xyz", None),
            P("ta", "grp", None, "xyz", None),
            P(),
        ),
        out_specs=(
            P("grp", None, "ta", "xyz", None),
            P("ta", "xyz", None, None, "grp"),
            P("ta", "xyz", "grp", None),
        ),
        check_vma=False,
    )
```

```python
import functools
import math

import jax
import jax.numpy as jnp
from jax import lax
from jax.experimental import pallas as pl
from jax.experimental.pallas import tpu as pltpu
from jax.sharding import PartitionSpec as P

MESH = pl.DeviceIdType.MESH
F32 = jnp.float32
BF16 = jnp.bfloat16
SX = 16
ITERS = 4
HOPPING = 0.1
GAMMA_TABLE = (
    ((3, 0, 1), (2, 0, 1), (1, 0, -1), (0, 0, -1)),
    ((3, -1, 0), (2, 1, 0), (1, 1, 0), (0, -1, 0)),
    ((2, 0, 1), (3, 0, -1), (0, 0, -1), (1, 0, 1)),
    ((2, 1, 0), (3, 1, 0), (0, 1, 0), (1, 1, 0)),
)


def dot_nt(a, b):
    return lax.dot_general(a, b, (((1,), (1,)), ((), ())), preferred_element_type=F32)


def plus(a, b, sign):
    return a + b if sign > 0 else a - b


def phased(re, im, pr, pi):
    if pi == 0:
        return (pr, re), (pr, im)
    return (-pi, im), (pi, re)


def project(psi, direction, sign):
    re, im = [], []
    for target in range(2):
        source, pr, pi = GAMMA_TABLE[direction][target]
        (s0, a0), (s1, a1) = phased(psi[source][0], psi[source][1], pr, pi)
        re.append(plus(psi[target][0], a0, sign * s0))
        im.append(plus(psi[target][1], a1, sign * s1))
    return jnp.stack(re), jnp.stack(im)


def rebuild(acc, re, im, direction, sign):
    for target in range(4):
        if target < 2:
            terms = ((1, re[target]), (1, im[target]))
        else:
            source, pr, pi = GAMMA_TABLE[direction][target]
            (s0, a0), (s1, a1) = phased(re[source], im[source], pr, pi)
            terms = ((sign * s0, a0), (sign * s1, a1))
        for part in range(2):
            s, a = terms[part]
            old = acc[target][part]
            if old is None:
                acc[target][part] = a if s > 0 else -a
            else:
                acc[target][part] = plus(old, a, s)


def colour(u, re, im, dagger):
    out_re = out_im = None
    for b in range(3):
        ur = u[0, b] if dagger else u[0, :, b]
        ui = u[1, b] if dagger else u[1, :, b]
        vr, vi = re[:, b][:, None], im[:, b][:, None]
        ur, ui = ur[None], ui[None]
        t0 = plus(ur * vr, ui * vi, 1 if dagger else -1)
        t1 = plus(ur * vi, ui * vr, -1 if dagger else 1)
        out_re = t0 if out_re is None else out_re + t0
        out_im = t1 if out_im is None else out_im + t1
    return out_re, out_im


def roll(v, shift, axis):
    shape = v.shape
    flat = v.reshape((-1,) + shape[-2:])
    return pltpu.roll(flat, shift % shape[axis - 2 + len(shape)], axis=1 + axis).reshape(shape)


def kernel(
    sizes, al_ref, rs_hbm, lk_hbm, v_hbm,
    sol_ref, cor_ref, per_ref,
    rs_v, lk_v, vraw, v32, vall, relay, u8, lz, uz,
    res, total, hsum, tsend, trecv, zsend, zrecv, w_ref, ub_ref, g_ref, s_ref,
    csend, crecv, psend, precv,
    t_ss, t_rs, z_ss, z_rs, vh_ss, vh_rs, uh_ss, uh_rs, loc_s,
    o_ss, o_rs, r_ss, r_rs, c_ss, c_rs, p_ss, p_rs,
):
    n_grp, n_ta, n_xyz, scale = sizes
    grp = lax.axis_index("grp")
    ta = lax.axis_index("ta")
    me = lax.axis_index("xyz")
    half_ta = n_ta // 2
    y = grp * 2 + ta // half_ta
    x = ta % half_ta

    def y_device(step):
        other = (y + step + 4) % 4
        return (other // 2, (other % 2) * half_ta + x, me)

    z_next = (grp, ta, (me + 1) % n_xyz)
    z_prev = (grp, ta, (me + n_xyz - 1) % n_xyz)
    t_next = (grp, (ta + 1) % n_ta, me)
    t_prev = (grp, (ta + n_ta - 1) % n_ta, me)

    barrier = pltpu.get_barrier_semaphore()
    for device in (y_device(1), y_device(-1), t_next, t_prev):
        pl.semaphore_signal(barrier, inc=1, device_id=device, device_id_type=MESH)

    @pl.loop(1, n_xyz)
    def _(o):
        pl.semaphore_signal(
            barrier, inc=1, device_id=(grp, ta, (me + o) % n_xyz), device_id_type=MESH
        )

    fetches = (
        pltpu.make_async_copy(lk_hbm, lk_v, loc_s.at[0]),
        pltpu.make_async_copy(rs_hbm, rs_v, loc_s.at[1]),
        pltpu.make_async_copy(v_hbm, vraw.at[0], loc_s.at[2]),
    )
    for copy in fetches:
        copy.start()

    def remote(src, dst, ss, rs, device):
        return pltpu.make_async_remote_copy(
            src_ref=src, dst_ref=dst, send_sem=ss, recv_sem=rs, device_id=device,
            device_id_type=MESH,
        )

    def way(c):
        return y_device(1 - 2 * ((c // 2) % 2))

    def own_copy(c):
        rows = pl.ds(pl.multiple_of(c * 384, 384), 384)
        return remote(v_hbm.at[rows], relay.at[c], o_ss.at[c], o_rs.at[c], way(c))

    pl.semaphore_wait(barrier, n_xyz - 1 + 4)
    own_copy(0).start()
    own_copy(2).start()

    lane = lax.broadcasted_iota(jnp.int32, (8, 128), 1)
    sub = lax.broadcasted_iota(jnp.int32, (8, 128), 0)
    column = lane % SX
    z_is0 = sub % 2 == 0

    def shift_x(v, step):
        if step > 0:
            return jnp.where(column == SX - 1, roll(v, SX - 1, 1), roll(v, -1, 1))
        return jnp.where(column == 0, roll(v, 1 - SX, 1), roll(v, 1, 1))

    def shift_y(v, step):
        a = roll(v, -step * SX, 1)
        keep = lane < 128 - SX if step > 0 else lane >= SX
        return jnp.where(keep, a, roll(a, 4, 0))

    def spins(ref):
        v = ref[...].reshape(24, 8, 128)
        return [[v[6 * s + 3 * p : 6 * s + 3 * p + 3] for p in range(2)] for s in range(4)]

    def put(ref, s, p, value):
        k = 8 * (6 * s + 3 * p)
        ref[k : k + 24, :] = value.reshape(24, 128)

    def links_of(d):
        return u8[144 * d : 144 * (d + 1), :].reshape(2, 3, 3, 8, 128)

    def t_copies(n):
        return (
            remote(tsend.at[n, 0], trecv.at[n, 0], t_ss.at[n, 0], t_rs.at[n, 0], t_prev),
            remote(tsend.at[n, 1], trecv.at[n, 1], t_ss.at[n, 1], t_rs.at[n, 1], t_next),
            remote(zsend.at[n, 0], zrecv.at[n, 0], z_ss.at[n, 0], z_rs.at[n, 0], z_prev),
            remote(zsend.at[n, 1], zrecv.at[n, 1], z_ss.at[n, 1], z_rs.at[n, 1], z_next),
        )

    def prepare(n):
        psi = spins(res)
        re, im = project(psi, 3, -1)
        tsend[n, 0, 0], tsend[n, 0, 1] = re, im
        re, im = colour(links_of(3), *project(psi, 3, 1), True)
        tsend[n, 1, 0], tsend[n, 1, 1] = re, im
        re, im = project(psi, 2, -1)
        zsend[n, 0, 0] = jnp.where(z_is0, re[0], roll(re[1], 1, 0))
        zsend[n, 0, 1] = jnp.where(z_is0, im[0], roll(im[1], 1, 0))
        re, im = colour(links_of(2), *project(psi, 2, 1), True)
        zsend[n, 1, 0] = jnp.where(z_is0, roll(re[1], 7, 0), re[0])
        zsend[n, 1, 1] = jnp.where(z_is0, roll(im[1], 7, 0), im[0])

    def local_hops():
        psi = spins(res)
        acc = [[None, None] for _ in range(4)]
        for d, shift in ((0, shift_x), (1, shift_y)):
            re, im = project(psi, d, -1)
            rebuild(acc, *colour(links_of(d), shift(re, 1), shift(im, 1), False), d, -1)
            re, im = colour(links_of(d), *project(psi, d, 1), True)
            rebuild(acc, shift(re, -1), shift(im, -1), d, 1)
        for s in range(4):
            for p in range(2):
                put(hsum, s, p, acc[s][p])

    def finish(n):
        psi = spins(res)
        acc = spins(hsum)
        sums = spins(total)
        sign_up = jnp.where(ta == n_ta - 1, -1.0, 1.0).astype(F32)
        sign_down = jnp.where(ta == 0, -1.0, 1.0).astype(F32)
        re, im = project(psi, 2, -1)

        def ahead(v, got):
            return jnp.where(z_is0, roll(v, 7, 0), jnp.stack([roll(got, 1, 0), got]))

        re, im = ahead(re, zrecv[n, 0, 0]), ahead(im, zrecv[n, 0, 1])
        rebuild(acc, *colour(links_of(2), re, im, False), 2, -1)
        re, im = colour(links_of(2), *project(psi, 2, 1), True)

        def behind(v, got):
            return jnp.where(z_is0, jnp.stack([roll(got, 7, 0), got]), roll(v, 1, 0))

        re, im = behind(re, zrecv[n, 1, 0]), behind(im, zrecv[n, 1, 1])
        rebuild(acc, re, im, 2, 1)
        re, im = trecv[n, 0, 0] * sign_up, trecv[n, 0, 1] * sign_up
        rebuild(acc, *colour(links_of(3), re, im, False), 3, -1)
        rebuild(acc, trecv[n, 1, 0] * sign_down, trecv[n, 1, 1] * sign_down, 3, 1)
        step = al_ref[n]
        step_after = al_ref[n + 1]
        for s in range(4):
            for p in range(2):
                old = psi[s][p]
                new = old - step * (old - HOPPING * acc[s][p])
                put(res, s, p, new)
                put(total, s, p, sums[s][p] + step_after * new)

    fetches[0].wait()
    fetches[1].wait()
    first_step = al_ref[0]
    for h in range(2):
        for z in range(2):
            links = lk_v[pl.ds(2 * h + z, 72, stride=4), :]
            for r in range(2):
                u8[pl.ds(4 * h + 2 * r + z, 72, stride=8), :] = links
                values = rs_v[pl.ds(96 * r + 2 * h + z, 24, stride=4), :]
                res[pl.ds(4 * h + 2 * r + z, 24, stride=8), :] = values
                total[pl.ds(4 * h + 2 * r + z, 24, stride=8), :] = first_step * values
            for d in range(3):
                rows = 0.5 * lk_v[pl.ds(72 * d + 2 * h + z, 18, stride=4), :]
                lz[z, d, :, 128 * h : 128 * (h + 1)] = rows
                if d == 2 and z == 1:
                    uz[:, 128 * h : 128 * (h + 1)] = rows
                if d == 2 and z == 0:
                    ub_ref[1, 2, :, 128 * h : 128 * (h + 1)] = rows
    lcol = lax.broadcasted_iota(jnp.int32, (18, 256), 1) % SX
    for z in range(2):
        links = lz[z, 0]
        ub_ref[z, 0] = jnp.where(
            lcol == 0, pltpu.roll(links, 256 - (SX - 1), axis=1), pltpu.roll(links, 1, axis=1)
        )
        ub_ref[z, 1] = pltpu.roll(lz[z, 1], SX, axis=1)

    def relay_copy(c):
        rows = pl.ds(pl.multiple_of(c * 384, 384), 384)
        return remote(relay.at[c], vraw.at[1, rows], r_ss.at[c], r_rs.at[c], way(c))

    def pass_on(step):
        for c in (step + 2 * (step // 2), step + 2 * (step // 2) + 2):
            own_copy(c).wait()
            relay_copy(c).start()

    def sort_chunk(which, c):
        v32[...] = vraw[which, pl.ds(pl.multiple_of(c * 384, 384), 384), :].astype(F32)
        rows = pl.ds(pl.multiple_of(c * 16, 16), 16)
        for m in range(6):
            for h in range(2):
                for z in range(2):
                    k = (z * 6 + m) * 256 + h * 128
                    vall[which, rows, k : k + 128] = v32[
                        pl.ds(4 * m + 2 * h + z, 16, stride=24), :
                    ].astype(BF16)

    low, high = vall.at[0, :, pl.ds(0, 1536)], vall.at[0, :, pl.ds(1536, 1536)]
    halo_copies = (
        remote(low, w_ref.at[1, 0], vh_ss.at[0], vh_rs.at[0], z_prev),
        remote(high, w_ref.at[0, 1], vh_ss.at[1], vh_rs.at[1], z_next),
        remote(uz, ub_ref.at[0, 2], uh_ss, uh_rs, z_next),
        pltpu.make_async_copy(high, w_ref.at[0, 0], loc_s.at[0]),
        pltpu.make_async_copy(low, w_ref.at[1, 1], loc_s.at[1]),
    )

    def gradient(d):
        @pl.loop(0, 4)
        def _(q):
            z, h = q // 2, q % 2
            lanes = pl.ds(pl.multiple_of(h * 128, 128), 128)
            lane16 = lax.broadcasted_iota(jnp.int32, (16, 128), 1)

            def part(m, side=h):
                return pl.ds(pl.multiple_of(m * 256 + side * 128, 128), 128)

            @pl.loop(0, 8, unroll=4)
            def _(kc):
                rows = pl.ds(pl.multiple_of(kc * 16, 16), 16)

                def own(m, side):
                    return vall[0, rows, part(z * 6 + m, side)]

                def neighbours(m):
                    if d == 0:
                        v = own(m, h)
                        column = lane16 % SX
                        return (
                            jnp.where(
                                column == SX - 1,
                                pltpu.roll(v, SX - 1, axis=1),
                                pltpu.roll(v, 127, axis=1),
                            ),
                            jnp.where(
                                column == 0,
                                pltpu.roll(v, 129 - SX, axis=1),
                                pltpu.roll(v, 1, axis=1),
                            ),
                        )
                    if d == 1:
                        v, w = own(m, h), own(m, 1 - h)
                        up, down = 128 - SX, SX
                        return (
                            jnp.where(
                                lane16 < up,
                                pltpu.roll(v, up, axis=1),
                                pltpu.roll(w, up, axis=1),
                            ),
                            jnp.where(
                                lane16 >= down,
                                pltpu.roll(v, down, axis=1),
                                pltpu.roll(w, down, axis=1),
                            ),
                        )
                    return tuple(w_ref[z, s, rows, part(m)] for s in range(2))

                both = [neighbours(m) for m in range(6)]
                outs = []
                for side in range(2):
                    v = [both[m][side].astype(F32) for m in range(6)]
                    l_ref = lz if side == 0 else ub_ref
                    u = [
                        jnp.broadcast_to(l_ref[z, d, i : i + 1, lanes], (16, 128))
                        for i in range(18)
                    ]
                    for a in range(3):
                        re = im = None
                        for b in range(3):
                            if side == 0:
                                ur, ui = u[3 * a + b], u[9 + 3 * a + b]
                                t0 = ur * v[b] - ui * v[3 + b]
                                t1 = ur * v[3 + b] + ui * v[b]
                            else:
                                ur, ui = u[3 * b + a], u[9 + 3 * b + a]
                                t0 = ur * v[b] + ui * v[3 + b]
                                t1 = ur * v[3 + b] - ui * v[b]
                            re = t0 if re is None else re + t0
                            im = t1 if im is None else im + t1
                        outs.append((re, im))
                above = pl.ds(pl.multiple_of(d * 256 + kc * 16, 16), 16)
                below = pl.ds(pl.multiple_of(d * 256 + 128 + kc * 16, 16), 16)
                for a in range(3):
                    re = (outs[a][0] - outs[3 + a][0]).astype(BF16)
                    im = (outs[a][1] - outs[3 + a][1]).astype(BF16)
                    g_ref[above, part(z * 6 + a)] = re
                    g_ref[above, part(z * 6 + 3 + a)] = im
                    g_ref[below, part(z * 6 + a)] = im
                    g_ref[below, part(z * 6 + 3 + a)] = -re

    def c_copy(target, o):
        return remote(
            csend.at[target], crecv.at[o], c_ss.at[o], c_rs.at[o], (grp, ta, target)
        )

    def p_copy(target, o):
        return remote(
            psend.at[target], precv.at[o], p_ss.at[o], p_rs.at[o], (grp, ta, target)
        )

    def send(copy_of, first, count):
        @pl.loop(0, count)
        def _(i):
            target = first + i
            o = (target - me + n_xyz) % n_xyz

            @pl.when(o != 0)
            def _():
                copy_of(target, o).start()

    def correlate(vectors, first):
        count = vectors.shape[0] // 16
        for d in range(3):
            c = dot_nt(g_ref[256 * d : 256 * (d + 1), :], vectors).T.astype(BF16)
            csend[pl.ds(first, count), :, 256 * d : 256 * (d + 1)] = c.reshape(count, 16, 256)
        send(c_copy, first, count)

    def overlap(vectors, first):
        count = vectors.shape[0] // 16
        p = dot_nt(vectors, s_ref[...]).reshape(2 * count, 8, 128)
        p = jnp.where((lane // 16 == sub)[None], p, 0.0)
        p = jnp.sum(p, axis=1, keepdims=True)
        psend[pl.ds(first, count)] = p.reshape(count, 2, 1, 128)
        send(p_copy, first, count)

    @pl.loop(0, ITERS - 1)
    def _(n):
        prepare(n)
        for copy in t_copies(n):
            copy.start()

        @pl.when(n == 0)
        def _():
            @pl.loop(2, 8)
            def _(i):
                own_copy(i // 4 * 4 + (i % 2) * 2 + (i // 2) % 2).start()

        local_hops()

        @pl.when(n == 0)
        def _():
            fetches[2].wait()

            @pl.loop(0, 8)
            def _(c):
                sort_chunk(0, c)

            for copy in halo_copies:
                copy.start()

            gradient(0)

        @pl.when(n == 1)
        def _():
            gradient(1)

        @pl.when(n == 2)
        def _():
            for copy in halo_copies:
                copy.wait()
            gradient(2)
            correlate(vall[0], grp * 8)

        pass_on(n)
        for copy in t_copies(n):
            copy.wait()
        finish(n)

    pass_on(3)

    row = lax.broadcasted_iota(jnp.int32, (96, 48), 0)
    col = lax.broadcasted_iota(jnp.int32, (96, 48), 1)
    row_m, row_r, row_p, row_s = row // 16, (row // 8) % 2, (row // 4) % 2, row % 4
    col_r, col_s, col_m = col // 24, (col // 6) % 4, col % 6
    same = (row_r == col_r) & (row_s == col_s)
    want = jnp.where(row_p == 0, row_m, (row_m + 3) % 6)
    value = jnp.where((row_p == 1) & (row_m >= 3), -1.0, 1.0)
    pick = jnp.where(same & (want == col_m), value, 0.0).astype(BF16)
    for z in range(2):
        rows = []
        for r in range(2):
            halves = []
            for h in range(2):
                here = pl.ds(4 * h + 2 * r + z, 24, stride=8)
                there = pl.ds(96 * r + 2 * h + z, 24, stride=4)
                values = total[here, :]
                sol_ref[there, :] = values
                halves.append(values)
            rows.append(jnp.concatenate(halves, axis=1))
        spinors = jnp.concatenate(rows, axis=0).astype(BF16)
        placed = jnp.dot(pick, spinors, preferred_element_type=F32).astype(BF16)
        for m in range(6):
            rows = placed[16 * m : 16 * m + 16]
            s_ref[:, (z * 6 + m) * 256 : (z * 6 + m + 1) * 256] = jnp.concatenate([rows] * 8)

    overlap(vall[0], grp * 8)

    @pl.loop(0, 2)
    def _(half):
        @pl.loop(0, 4)
        def _(j):
            relay_copy(4 * half + j).wait()
            sort_chunk(1, 4 * half + j)

        first = (1 - grp) * 8 + half * 4
        vectors = vall[1, pl.ds(pl.multiple_of(half * 64, 64), 64), :]
        correlate(vectors, first)
        overlap(vectors, first)

    @pl.loop(1, n_xyz)
    def _(o):
        target = (me + o) % n_xyz
        c_copy(target, o).wait()
        p_copy(target, o).wait()

    c_sum = csend[me].astype(F32)
    p_sum = psend[me]
    for o in range(1, n_xyz):
        c_sum = c_sum + crecv[o].astype(F32)
        p_sum = p_sum + precv[o]
    for k in range(6):
        cor_ref[pl.ds(k, 16, stride=6), :] = c_sum[:, 128 * k : 128 * (k + 1)] * scale
    p_sum = p_sum * scale
    tall = []
    for i in range(2):
        wide = jnp.broadcast_to(p_sum[i], (8, 128))
        rows = wide
        for j in range(1, 8):
            rows = jnp.where(sub == j, pltpu.roll(wide, 128 - 16 * j, axis=1), rows)
        tall.append(rows)
    wide = jnp.concatenate(tall + [jnp.zeros((112, 128), F32)], axis=0).T
    per_ref[0] = wide[0:8, 0:16]
    per_ref[1] = wide[8:16, 0:16]


def rows_of(array, lead):
    return array.reshape(lead, 2, 2, 128).transpose(0, 2, 1, 3).reshape(lead * 4, 128)


def body(sizes, right_sides, gauge_links, eigenvectors, step_lengths):
    vmem = pl.BlockSpec(memory_space=pltpu.VMEM)
    anywhere = pl.BlockSpec(memory_space=pl.ANY)
    n_it = ITERS - 1
    dma = pltpu.SemaphoreType.DMA
    sol, cor, per = pl.pallas_call(
        functools.partial(kernel, sizes),
        out_shape=(
            pltpu.VMEM((192, 128), F32),
            pltpu.VMEM((96, 128), F32),
            pltpu.VMEM((2, 8, 16), F32),
        ),
        in_specs=[pl.BlockSpec(memory_space=pltpu.SMEM), anywhere, anywhere, anywhere],
        out_specs=(vmem, vmem, vmem),
        scratch_shapes=[
            pltpu.VMEM((192, 128), F32),
            pltpu.VMEM((288, 128), F32),
            pltpu.VMEM((2, 3072, 128), BF16),
            pltpu.VMEM((384, 128), F32),
            pltpu.VMEM((2, 128, 3072), BF16),
            pltpu.VMEM((8, 384, 128), BF16),
            pltpu.VMEM((576, 128), F32),
            pltpu.VMEM((2, 3, 18, 256), F32),
            pltpu.VMEM((18, 256), F32),
            pltpu.VMEM((192, 128), F32),
            pltpu.VMEM((192, 128), F32),
            pltpu.VMEM((192, 128), F32),
            pltpu.VMEM((n_it, 2, 2, 2, 3, 8, 128), F32),
            pltpu.VMEM((n_it, 2, 2, 2, 3, 8, 128), F32),
            pltpu.VMEM((n_it, 2, 2, 3, 8, 128), F32),
            pltpu.VMEM((n_it, 2, 2, 3, 8, 128), F32),
            pltpu.VMEM((2, 2, 128, 1536), BF16),
            pltpu.VMEM((2, 3, 18, 256), F32),
            pltpu.VMEM((768, 3072), BF16),
            pltpu.VMEM((128, 3072), BF16),
            pltpu.VMEM((16, 16, 768), BF16),
            pltpu.VMEM((16, 16, 768), BF16),
            pltpu.VMEM((16, 2, 1, 128), F32),
            pltpu.VMEM((16, 2, 1, 128), F32),
            dma((n_it, 2)), dma((n_it, 2)), dma((n_it, 2)), dma((n_it, 2)),
            dma((2,)), dma((2,)), dma(()), dma(()), dma((3,)),
            dma((8,)), dma((8,)), dma((8,)), dma((8,)),
            dma((16,)), dma((16,)), dma((16,)), dma((16,)),
        ],
        compiler_params=pltpu.CompilerParams(
            collective_id=0, has_side_effects=True, vmem_limit_bytes=56 * 1024 * 1024
        ),
    )(
        step_lengths,
        rows_of(right_sides, 48),
        rows_of(gauge_links, 72),
        rows_of(eigenvectors, 768),
    )
    sol = sol.reshape(48, 2, 2, 128).transpose(0, 2, 1, 3).reshape(right_sides.shape)
    cor = cor.reshape(1, 16, 3, 2, 128)
    return sol, cor, per.transpose(2, 0, 1)[None]


def solution(mesh):
    n_grp, n_ta, n_xyz = (mesh.shape[a] for a in ("grp", "ta", "xyz"))
    scale = 1.0 / math.sqrt(2 * n_xyz * 256)
    return jax.shard_map(
        functools.partial(body, (n_grp, n_ta, n_xyz, scale)),
        mesh=mesh,
        in_specs=(
            P("grp", None, "ta", "xyz", None),
            P(None, None, "ta", "xyz", None),
            P("ta", "grp", None, "xyz", None),
            P(),
        ),
        out_specs=(
            P("grp", None, "ta", "xyz", None),
            P("ta", "xyz", None, None, "grp"),
            P("ta", "xyz", "grp", None),
        ),
        check_vma=False,
    )
```

```python
import functools
import math

import jax
import jax.numpy as jnp
from jax import lax
from jax.experimental import pallas as pl
from jax.experimental.pallas import tpu as pltpu
from jax.sharding import PartitionSpec as P

MESH = pl.DeviceIdType.MESH
F32 = jnp.float32
BF16 = jnp.bfloat16
SX = 16
ITERS = 4
HOPPING = 0.1
GAMMA_TABLE = (
    ((3, 0, 1), (2, 0, 1), (1, 0, -1), (0, 0, -1)),
    ((3, -1, 0), (2, 1, 0), (1, 1, 0), (0, -1, 0)),
    ((2, 0, 1), (3, 0, -1), (0, 0, -1), (1, 0, 1)),
    ((2, 1, 0), (3, 1, 0), (0, 1, 0), (1, 1, 0)),
)


def dot_nt(a, b):
    return lax.dot_general(a, b, (((1,), (1,)), ((), ())), preferred_element_type=F32)


def plus(a, b, sign):
    return a + b if sign > 0 else a - b


def phased(re, im, pr, pi):
    if pi == 0:
        return (pr, re), (pr, im)
    return (-pi, im), (pi, re)


def project(psi, direction, sign):
    re, im = [], []
    for target in range(2):
        source, pr, pi = GAMMA_TABLE[direction][target]
        (s0, a0), (s1, a1) = phased(psi[source][0], psi[source][1], pr, pi)
        re.append(plus(psi[target][0], a0, sign * s0))
        im.append(plus(psi[target][1], a1, sign * s1))
    return jnp.stack(re), jnp.stack(im)


def rebuild(acc, re, im, direction, sign):
    for target in range(4):
        if target < 2:
            terms = ((1, re[target]), (1, im[target]))
        else:
            source, pr, pi = GAMMA_TABLE[direction][target]
            (s0, a0), (s1, a1) = phased(re[source], im[source], pr, pi)
            terms = ((sign * s0, a0), (sign * s1, a1))
        for part in range(2):
            s, a = terms[part]
            old = acc[target][part]
            if old is None:
                acc[target][part] = a if s > 0 else -a
            else:
                acc[target][part] = plus(old, a, s)


def colour(u, re, im, dagger):
    out_re = out_im = None
    for b in range(3):
        ur = u[0, b] if dagger else u[0, :, b]
        ui = u[1, b] if dagger else u[1, :, b]
        vr, vi = re[:, b][:, None], im[:, b][:, None]
        ur, ui = ur[None], ui[None]
        t0 = plus(ur * vr, ui * vi, 1 if dagger else -1)
        t1 = plus(ur * vi, ui * vr, -1 if dagger else 1)
        out_re = t0 if out_re is None else out_re + t0
        out_im = t1 if out_im is None else out_im + t1
    return out_re, out_im


def roll(v, shift, axis):
    shape = v.shape
    flat = v.reshape((-1,) + shape[-2:])
    return pltpu.roll(flat, shift % shape[axis - 2 + len(shape)], axis=1 + axis).reshape(shape)


def kernel(
    sizes, al_ref, rs_hbm, lk_hbm, v_hbm,
    sol_ref, cor_ref, per_ref,
    rs_v, lk_v, vraw, v32, vall, relay, u8, lz, uz,
    res, total, hsum, tsend, trecv, zsend, zrecv, w_ref, ub_ref, g_ref, s_ref,
    cpart, csib, cmsg, cown, crecv, psend, precv, pwork,
    t_ss, t_rs, z_ss, z_rs, vh_ss, vh_rs, uh_ss, uh_rs, loc_s,
    o_ss, o_rs, r_ss, r_rs, b_ss, b_rs, c_ss, c_rs, p_ss, p_rs,
):
    n_grp, n_ta, n_xyz, scale = sizes
    grp = lax.axis_index("grp")
    ta = lax.axis_index("ta")
    me = lax.axis_index("xyz")
    chip, core = me // 2, me % 2
    n_chip = n_xyz // 2
    half_ta = n_ta // 2
    y = grp * 2 + ta // half_ta
    x = ta % half_ta

    def y_device(step):
        other = (y + step + 4) % 4
        return (other // 2, (other % 2) * half_ta + x, me)

    z_next = (grp, ta, (me + 1) % n_xyz)
    z_prev = (grp, ta, (me + n_xyz - 1) % n_xyz)
    t_next = (grp, (ta + 1) % n_ta, me)
    t_prev = (grp, (ta + n_ta - 1) % n_ta, me)

    barrier = pltpu.get_barrier_semaphore()
    for device in (y_device(1), y_device(-1), t_next, t_prev):
        pl.semaphore_signal(barrier, inc=1, device_id=device, device_id_type=MESH)

    @pl.loop(1, n_xyz)
    def _(o):
        pl.semaphore_signal(
            barrier, inc=1, device_id=(grp, ta, (me + o) % n_xyz), device_id_type=MESH
        )

    fetches = (
        pltpu.make_async_copy(lk_hbm, lk_v, loc_s.at[0]),
        pltpu.make_async_copy(rs_hbm, rs_v, loc_s.at[1]),
        pltpu.make_async_copy(v_hbm, vraw.at[0], loc_s.at[2]),
    )
    for copy in fetches:
        copy.start()

    def remote(src, dst, ss, rs, device):
        return pltpu.make_async_remote_copy(
            src_ref=src, dst_ref=dst, send_sem=ss, recv_sem=rs, device_id=device,
            device_id_type=MESH,
        )

    def way(c):
        return y_device(1 - 2 * (c % 2))

    def own_copy(c):
        rows = pl.ds(pl.multiple_of(c * 384, 384), 384)
        return remote(v_hbm.at[rows], relay.at[c], o_ss.at[c], o_rs.at[c], way(c))

    pl.semaphore_wait(barrier, n_xyz - 1 + 4)
    own_copy(0).start()
    own_copy(1).start()

    lane = lax.broadcasted_iota(jnp.int32, (8, 128), 1)
    sub = lax.broadcasted_iota(jnp.int32, (8, 128), 0)
    column = lane % SX
    z_is0 = sub % 2 == 0

    def shift_x(v, step):
        if step > 0:
            return jnp.where(column == SX - 1, roll(v, SX - 1, 1), roll(v, -1, 1))
        return jnp.where(column == 0, roll(v, 1 - SX, 1), roll(v, 1, 1))

    def shift_y(v, step):
        a = roll(v, -step * SX, 1)
        keep = lane < 128 - SX if step > 0 else lane >= SX
        return jnp.where(keep, a, roll(a, 4, 0))

    def spins(ref):
        v = ref[...].reshape(24, 8, 128)
        return [[v[6 * s + 3 * p : 6 * s + 3 * p + 3] for p in range(2)] for s in range(4)]

    def put(ref, s, p, value):
        k = 8 * (6 * s + 3 * p)
        ref[k : k + 24, :] = value.reshape(24, 128)

    def links_of(d):
        return u8[144 * d : 144 * (d + 1), :].reshape(2, 3, 3, 8, 128)

    def t_copies(n):
        return (
            remote(tsend.at[n, 0], trecv.at[n, 0], t_ss.at[n, 0], t_rs.at[n, 0], t_prev),
            remote(tsend.at[n, 1], trecv.at[n, 1], t_ss.at[n, 1], t_rs.at[n, 1], t_next),
            remote(zsend.at[n, 0], zrecv.at[n, 0], z_ss.at[n, 0], z_rs.at[n, 0], z_prev),
            remote(zsend.at[n, 1], zrecv.at[n, 1], z_ss.at[n, 1], z_rs.at[n, 1], z_next),
        )

    def prepare(n):
        psi = spins(res)
        re, im = project(psi, 3, -1)
        tsend[n, 0, 0], tsend[n, 0, 1] = re, im
        re, im = colour(links_of(3), *project(psi, 3, 1), True)
        tsend[n, 1, 0], tsend[n, 1, 1] = re, im
        re, im = project(psi, 2, -1)
        zsend[n, 0, 0] = jnp.where(z_is0, re[0], roll(re[1], 1, 0))
        zsend[n, 0, 1] = jnp.where(z_is0, im[0], roll(im[1], 1, 0))
        re, im = colour(links_of(2), *project(psi, 2, 1), True)
        zsend[n, 1, 0] = jnp.where(z_is0, roll(re[1], 7, 0), re[0])
        zsend[n, 1, 1] = jnp.where(z_is0, roll(im[1], 7, 0), im[0])

    def local_hops():
        psi = spins(res)
        acc = [[None, None] for _ in range(4)]
        for d, shift in ((0, shift_x), (1, shift_y)):
            re, im = project(psi, d, -1)
            rebuild(acc, *colour(links_of(d), shift(re, 1), shift(im, 1), False), d, -1)
            re, im = colour(links_of(d), *project(psi, d, 1), True)
            rebuild(acc, shift(re, -1), shift(im, -1), d, 1)
        for s in range(4):
            for p in range(2):
                put(hsum, s, p, acc[s][p])

    def finish(n):
        psi = spins(res)
        acc = spins(hsum)
        sums = spins(total)
        sign_up = jnp.where(ta == n_ta - 1, -1.0, 1.0).astype(F32)
        sign_down = jnp.where(ta == 0, -1.0, 1.0).astype(F32)
        re, im = project(psi, 2, -1)

        def ahead(v, got):
            return jnp.where(z_is0, roll(v, 7, 0), jnp.stack([roll(got, 1, 0), got]))

        re, im = ahead(re, zrecv[n, 0, 0]), ahead(im, zrecv[n, 0, 1])
        rebuild(acc, *colour(links_of(2), re, im, False), 2, -1)
        re, im = colour(links_of(2), *project(psi, 2, 1), True)

        def behind(v, got):
            return jnp.where(z_is0, jnp.stack([roll(got, 7, 0), got]), roll(v, 1, 0))

        re, im = behind(re, zrecv[n, 1, 0]), behind(im, zrecv[n, 1, 1])
        rebuild(acc, re, im, 2, 1)
        re, im = trecv[n, 0, 0] * sign_up, trecv[n, 0, 1] * sign_up
        rebuild(acc, *colour(links_of(3), re, im, False), 3, -1)
        rebuild(acc, trecv[n, 1, 0] * sign_down, trecv[n, 1, 1] * sign_down, 3, 1)
        step = al_ref[n]
        step_after = al_ref[n + 1]
        for s in range(4):
            for p in range(2):
                old = psi[s][p]
                new = old - step * (old - HOPPING * acc[s][p])
                put(res, s, p, new)
                put(total, s, p, sums[s][p] + step_after * new)

    vall[256:352, :] = jnp.zeros((96, 3072), BF16)

    fetches[0].wait()
    fetches[1].wait()
    first_step = al_ref[0]
    for h in range(2):
        for z in range(2):
            links = lk_v[pl.ds(2 * h + z, 72, stride=4), :]
            for r in range(2):
                u8[pl.ds(4 * h + 2 * r + z, 72, stride=8), :] = links
                values = rs_v[pl.ds(96 * r + 2 * h + z, 24, stride=4), :]
                res[pl.ds(4 * h + 2 * r + z, 24, stride=8), :] = values
                total[pl.ds(4 * h + 2 * r + z, 24, stride=8), :] = first_step * values
            for d in range(3):
                rows = 0.5 * lk_v[pl.ds(72 * d + 2 * h + z, 18, stride=4), :]
                lz[z, d, :, 128 * h : 128 * (h + 1)] = rows
                if d == 2 and z == 1:
                    uz[:, 128 * h : 128 * (h + 1)] = rows
                if d == 2 and z == 0:
                    ub_ref[1, 2, :, 128 * h : 128 * (h + 1)] = rows
    lcol = lax.broadcasted_iota(jnp.int32, (18, 256), 1) % SX
    for z in range(2):
        links = lz[z, 0]
        ub_ref[z, 0] = jnp.where(
            lcol == 0, pltpu.roll(links, 256 - (SX - 1), axis=1), pltpu.roll(links, 1, axis=1)
        )
        ub_ref[z, 1] = pltpu.roll(lz[z, 1], SX, axis=1)

    def relay_copy(c):
        rows = pl.ds(pl.multiple_of(c * 384, 384), 384)
        return remote(relay.at[c], vraw.at[1, rows], r_ss.at[c], r_rs.at[c], way(c))

    def pass_on(step):
        for c in (2 * step, 2 * step + 1):
            own_copy(c).wait()
            relay_copy(c).start()

    def sort_chunk(which, c):
        v32[...] = vraw[which, pl.ds(pl.multiple_of(c * 384, 384), 384), :].astype(F32)
        rows = pl.ds(pl.multiple_of(which * 128 + c * 16, 16), 16)
        for m in range(6):
            for h in range(2):
                for z in range(2):
                    k = (z * 6 + m) * 256 + h * 128
                    vall[rows, k : k + 128] = v32[
                        pl.ds(4 * m + 2 * h + z, 16, stride=24), :
                    ].astype(BF16)

    own = pl.ds(0, 128)
    low, high = vall.at[own, pl.ds(0, 1536)], vall.at[own, pl.ds(1536, 1536)]
    halo_copies = (
        remote(low, w_ref.at[1, 0], vh_ss.at[0], vh_rs.at[0], z_prev),
        remote(high, w_ref.at[0, 1], vh_ss.at[1], vh_rs.at[1], z_next),
        remote(uz, ub_ref.at[0, 2], uh_ss, uh_rs, z_next),
        pltpu.make_async_copy(high, w_ref.at[0, 0], loc_s.at[0]),
        pltpu.make_async_copy(low, w_ref.at[1, 1], loc_s.at[1]),
    )

    def gradient(d):
        @pl.loop(0, 4)
        def _(q):
            z, h = q // 2, q % 2
            lanes = pl.ds(pl.multiple_of(h * 128, 128), 128)
            lane16 = lax.broadcasted_iota(jnp.int32, (16, 128), 1)

            def part(m, side=h):
                return pl.ds(pl.multiple_of(m * 256 + side * 128, 128), 128)

            @pl.loop(0, 8, unroll=4)
            def _(kc):
                rows = pl.ds(pl.multiple_of(kc * 16, 16), 16)

                def here(m, side):
                    return vall[rows, part(z * 6 + m, side)]

                def neighbours(m):
                    if d == 0:
                        v = here(m, h)
                        column = lane16 % SX
                        return (
                            jnp.where(
                                column == SX - 1,
                                pltpu.roll(v, SX - 1, axis=1),
                                pltpu.roll(v, 127, axis=1),
                            ),
                            jnp.where(
                                column == 0,
                                pltpu.roll(v, 129 - SX, axis=1),
                                pltpu.roll(v, 1, axis=1),
                            ),
                        )
                    if d == 1:
                        v, w = here(m, h), here(m, 1 - h)
                        up, down = 128 - SX, SX
                        return (
                            jnp.where(
                                lane16 < up,
                                pltpu.roll(v, up, axis=1),
                                pltpu.roll(w, up, axis=1),
                            ),
                            jnp.where(
                                lane16 >= down,
                                pltpu.roll(v, down, axis=1),
                                pltpu.roll(w, down, axis=1),
                            ),
                        )
                    return tuple(w_ref[z, s, rows, part(m)] for s in range(2))

                both = [neighbours(m) for m in range(6)]
                outs = []
                for side in range(2):
                    v = [both[m][side].astype(F32) for m in range(6)]
                    l_ref = lz if side == 0 else ub_ref
                    u = [
                        jnp.broadcast_to(l_ref[z, d, i : i + 1, lanes], (16, 128))
                        for i in range(18)
                    ]
                    for a in range(3):
                        re = im = None
                        for b in range(3):
                            if side == 0:
                                ur, ui = u[3 * a + b], u[9 + 3 * a + b]
                                t0 = ur * v[b] - ui * v[3 + b]
                                t1 = ur * v[3 + b] + ui * v[b]
                            else:
                                ur, ui = u[3 * b + a], u[9 + 3 * b + a]
                                t0 = ur * v[b] + ui * v[3 + b]
                                t1 = ur * v[3 + b] - ui * v[b]
                            re = t0 if re is None else re + t0
                            im = t1 if im is None else im + t1
                        outs.append((re, im))
                above = pl.ds(pl.multiple_of(d * 256 + kc * 16, 16), 16)
                below = pl.ds(pl.multiple_of(d * 256 + 128 + kc * 16, 16), 16)
                for a in range(3):
                    re = (outs[a][0] - outs[3 + a][0]).astype(BF16)
                    im = (outs[a][1] - outs[3 + a][1]).astype(BF16)
                    g_ref[above, part(z * 6 + a)] = re
                    g_ref[above, part(z * 6 + 3 + a)] = im
                    g_ref[below, part(z * 6 + a)] = im
                    g_ref[below, part(z * 6 + 3 + a)] = -re

    def sibling_copy(k, i):
        return remote(
            cpart.at[2 * k + 1 - core], csib.at[i], b_ss.at[i], b_rs.at[i],
            (grp, ta, me + 1 - 2 * core),
        )

    def c_copy(i):
        o = (i - chip + n_chip) % n_chip
        return remote(
            cmsg.at[i], crecv.at[o], c_ss.at[o], c_rs.at[o], (grp, ta, 2 * i + core)
        )

    def p_copy(target, o):
        return remote(
            psend.at[target], precv.at[o], p_ss.at[o], p_rs.at[o], (grp, ta, target)
        )

    @pl.loop(0, ITERS - 1)
    def _(n):
        prepare(n)
        for copy in t_copies(n):
            copy.start()

        @pl.when(n == 0)
        def _():
            @pl.loop(2, 8)
            def _(i):
                own_copy(i).start()

        local_hops()

        @pl.when(n == 0)
        def _():
            fetches[2].wait()

            @pl.loop(0, 8)
            def _(c):
                sort_chunk(0, c)

            for copy in halo_copies:
                copy.start()

            gradient(0)

        @pl.when(n == 1)
        def _():
            gradient(1)

        @pl.when(n == 2)
        def _():
            pass_on(2)
            for copy in halo_copies:
                copy.wait()
            gradient(2)

        pass_on(n + n // 2)
        for copy in t_copies(n):
            copy.wait()
        finish(n)

    row = lax.broadcasted_iota(jnp.int32, (96, 48), 0)
    col = lax.broadcasted_iota(jnp.int32, (96, 48), 1)
    row_m, row_r, row_p, row_s = row // 16, (row // 8) % 2, (row // 4) % 2, row % 4
    col_r, col_s, col_m = col // 24, (col // 6) % 4, col % 6
    same = (row_r == col_r) & (row_s == col_s)
    want = jnp.where(row_p == 0, row_m, (row_m + 3) % 6)
    value = jnp.where((row_p == 1) & (row_m >= 3), -1.0, 1.0)
    pick = jnp.where(same & (want == col_m), value, 0.0).astype(BF16)
    for z in range(2):
        rows = []
        for r in range(2):
            halves = []
            for h in range(2):
                here = pl.ds(4 * h + 2 * r + z, 24, stride=8)
                there = pl.ds(96 * r + 2 * h + z, 24, stride=4)
                values = total[here, :]
                sol_ref[there, :] = values
                halves.append(values)
            rows.append(jnp.concatenate(halves, axis=1))
        spinors = jnp.concatenate(rows, axis=0).astype(BF16)
        placed = jnp.dot(pick, spinors, preferred_element_type=F32).astype(BF16)
        for m in range(6):
            rows = placed[16 * m : 16 * m + 16]
            s_ref[:, (z * 6 + m) * 256 : (z * 6 + m + 1) * 256] = jnp.concatenate([rows] * 8)

    @pl.loop(0, 3)
    def _(phase):
        late = phase // 2
        start, count = 6 * late, 8 - 2 * phase - 2 * late

        @pl.when(phase > 0)
        def _():
            @pl.loop(start, start + count)
            def _(c):
                relay_copy(c).wait()
                sort_chunk(1, c)

        half = jnp.where(phase == 0, grp, 1 - grp)
        first = half * 8 + start
        vectors = vall[pl.ds(pl.multiple_of(128 * phase - 32 * late, 32), 128), :]
        for d in range(3):
            c = dot_nt(g_ref[256 * d : 256 * (d + 1), :], vectors).T
            cpart[:, :, 256 * d : 256 * (d + 1)] = c.reshape(8, 16, 256)

        @pl.loop(0, count // 2)
        def _(k):
            sibling_copy(k, first // 2 + k).start()

        p = dot_nt(vectors, s_ref[...]).reshape(16, 8, 128)
        p = jnp.where((lane // 16 == sub)[None], p, 0.0)
        p = jnp.sum(p, axis=1, keepdims=True)
        pwork[...] = p.reshape(8, 2, 1, 128)

        @pl.loop(0, count)
        def _(k):
            target = first + k
            o = (target - me + n_xyz) % n_xyz
            psend[target] = pwork[k]

            @pl.when(o != 0)
            def _():
                p_copy(target, o).start()

        @pl.loop(0, count // 2)
        def _(k):
            i = first // 2 + k
            sibling_copy(k, i).wait()
            both = cpart[2 * k + core] + csib[i]

            @pl.when(i == chip)
            def _():
                cown[...] = both

            @pl.when(i != chip)
            def _():
                cmsg[i] = both.astype(BF16)
                c_copy(i).start()

    @pl.loop(1, n_xyz)
    def _(o):
        p_copy((me + o) % n_xyz, o).wait()

    @pl.loop(1, n_chip)
    def _(o):
        c_copy((chip + o) % n_chip).wait()

    c_sum = cown[...]
    for o in range(1, n_chip):
        c_sum = c_sum + crecv[o].astype(F32)
    p_sum = psend[me]
    for o in range(1, n_xyz):
        p_sum = p_sum + precv[o]
    for k in range(6):
        cor_ref[pl.ds(k, 16, stride=6), :] = c_sum[:, 128 * k : 128 * (k + 1)] * scale
    p_sum = p_sum * scale
    tall = []
    for i in range(2):
        wide = jnp.broadcast_to(p_sum[i], (8, 128))
        rows = wide
        for j in range(1, 8):
            rows = jnp.where(sub == j, pltpu.roll(wide, 128 - 16 * j, axis=1), rows)
        tall.append(rows)
    wide = jnp.concatenate(tall + [jnp.zeros((112, 128), F32)], axis=0).T
    per_ref[0] = wide[0:8, 0:16]
    per_ref[1] = wide[8:16, 0:16]


def rows_of(array, lead):
    return array.reshape(lead, 2, 2, 128).transpose(0, 2, 1, 3).reshape(lead * 4, 128)


def body(sizes, right_sides, gauge_links, eigenvectors, step_lengths):
    vmem = pl.BlockSpec(memory_space=pltpu.VMEM)
    anywhere = pl.BlockSpec(memory_space=pl.ANY)
    n_it = ITERS - 1
    dma = pltpu.SemaphoreType.DMA
    sol, cor, per = pl.pallas_call(
        functools.partial(kernel, sizes),
        out_shape=(
            pltpu.VMEM((192, 128), F32),
            pltpu.VMEM((96, 128), F32),
            pltpu.VMEM((2, 8, 16), F32),
        ),
        in_specs=[pl.BlockSpec(memory_space=pltpu.SMEM), anywhere, anywhere, anywhere],
        out_specs=(vmem, vmem, vmem),
        scratch_shapes=[
            pltpu.VMEM((192, 128), F32),
            pltpu.VMEM((288, 128), F32),
            pltpu.VMEM((2, 3072, 128), BF16),
            pltpu.VMEM((384, 128), F32),
            pltpu.VMEM((352, 3072), BF16),
            pltpu.VMEM((8, 384, 128), BF16),
            pltpu.VMEM((576, 128), F32),
            pltpu.VMEM((2, 3, 18, 256), F32),
            pltpu.VMEM((18, 256), F32),
            pltpu.VMEM((192, 128), F32),
            pltpu.VMEM((192, 128), F32),
            pltpu.VMEM((192, 128), F32),
            pltpu.VMEM((n_it, 2, 2, 2, 3, 8, 128), F32),
            pltpu.VMEM((n_it, 2, 2, 2, 3, 8, 128), F32),
            pltpu.VMEM((n_it, 2, 2, 3, 8, 128), F32),
            pltpu.VMEM((n_it, 2, 2, 3, 8, 128), F32),
            pltpu.VMEM((2, 2, 128, 1536), BF16),
            pltpu.VMEM((2, 3, 18, 256), F32),
            pltpu.VMEM((768, 3072), BF16),
            pltpu.VMEM((128, 3072), BF16),
            pltpu.VMEM((8, 16, 768), F32),
            pltpu.VMEM((8, 16, 768), F32),
            pltpu.VMEM((8, 16, 768), BF16),
            pltpu.VMEM((16, 768), F32),
            pltpu.VMEM((8, 16, 768), BF16),
            pltpu.VMEM((16, 2, 1, 128), F32),
            pltpu.VMEM((16, 2, 1, 128), F32),
            pltpu.VMEM((8, 2, 1, 128), F32),
            dma((n_it, 2)), dma((n_it, 2)), dma((n_it, 2)), dma((n_it, 2)),
            dma((2,)), dma((2,)), dma(()), dma(()), dma((3,)),
            dma((8,)), dma((8,)), dma((8,)), dma((8,)),
            dma((8,)), dma((8,)), dma((8,)), dma((8,)), dma((16,)), dma((16,)),
        ],
        compiler_params=pltpu.CompilerParams(
            collective_id=0, has_side_effects=True, vmem_limit_bytes=56 * 1024 * 1024
        ),
    )(
        step_lengths,
        rows_of(right_sides, 48),
        rows_of(gauge_links, 72),
        rows_of(eigenvectors, 768),
    )
    sol = sol.reshape(48, 2, 2, 128).transpose(0, 2, 1, 3).reshape(right_sides.shape)
    cor = cor.reshape(1, 16, 3, 2, 128)
    return sol, cor, per.transpose(2, 0, 1)[None]


def solution(mesh):
    n_grp, n_ta, n_xyz = (mesh.shape[a] for a in ("grp", "ta", "xyz"))
    scale = 1.0 / math.sqrt(2 * n_xyz * 256)
    return jax.shard_map(
        functools.partial(body, (n_grp, n_ta, n_xyz, scale)),
        mesh=mesh,
        in_specs=(
            P("grp", None, "ta", "xyz", None),
            P(None, None, "ta", "xyz", None),
            P("ta", "grp", None, "xyz", None),
            P(),
        ),
        out_specs=(
            P("grp", None, "ta", "xyz", None),
            P("ta", "xyz", None, None, "grp"),
            P("ta", "xyz", "grp", None),
        ),
        check_vma=False,
    )
```

```python
import functools
import math

import jax
import jax.numpy as jnp
from jax import lax
from jax.experimental import pallas as pl
from jax.experimental.pallas import tpu as pltpu
from jax.sharding import PartitionSpec as P

MESH = pl.DeviceIdType.MESH
F32 = jnp.float32
BF16 = jnp.bfloat16
SX = 16
ITERS = 4
HOPPING = 0.1
GAMMA_TABLE = (
    ((3, 0, 1), (2, 0, 1), (1, 0, -1), (0, 0, -1)),
    ((3, -1, 0), (2, 1, 0), (1, 1, 0), (0, -1, 0)),
    ((2, 0, 1), (3, 0, -1), (0, 0, -1), (1, 0, 1)),
    ((2, 1, 0), (3, 1, 0), (0, 1, 0), (1, 1, 0)),
)


def dot_nt(a, b):
    return lax.dot_general(a, b, (((1,), (1,)), ((), ())), preferred_element_type=F32)


def plus(a, b, sign):
    return a + b if sign > 0 else a - b


def phased(re, im, pr, pi):
    if pi == 0:
        return (pr, re), (pr, im)
    return (-pi, im), (pi, re)


def project(psi, direction, sign):
    re, im = [], []
    for target in range(2):
        source, pr, pi = GAMMA_TABLE[direction][target]
        (s0, a0), (s1, a1) = phased(psi[source][0], psi[source][1], pr, pi)
        re.append(plus(psi[target][0], a0, sign * s0))
        im.append(plus(psi[target][1], a1, sign * s1))
    return jnp.stack(re), jnp.stack(im)


def rebuild(acc, re, im, direction, sign):
    for target in range(4):
        if target < 2:
            terms = ((1, re[target]), (1, im[target]))
        else:
            source, pr, pi = GAMMA_TABLE[direction][target]
            (s0, a0), (s1, a1) = phased(re[source], im[source], pr, pi)
            terms = ((sign * s0, a0), (sign * s1, a1))
        for part in range(2):
            s, a = terms[part]
            old = acc[target][part]
            if old is None:
                acc[target][part] = a if s > 0 else -a
            else:
                acc[target][part] = plus(old, a, s)


def colour(u, re, im, dagger):
    out_re = out_im = None
    for b in range(3):
        ur = u[0, b] if dagger else u[0, :, b]
        ui = u[1, b] if dagger else u[1, :, b]
        vr, vi = re[:, b][:, None], im[:, b][:, None]
        ur, ui = ur[None], ui[None]
        t0 = plus(ur * vr, ui * vi, 1 if dagger else -1)
        t1 = plus(ur * vi, ui * vr, -1 if dagger else 1)
        out_re = t0 if out_re is None else out_re + t0
        out_im = t1 if out_im is None else out_im + t1
    return out_re, out_im


def roll(v, shift, axis):
    shape = v.shape
    flat = v.reshape((-1,) + shape[-2:])
    return pltpu.roll(flat, shift % shape[axis - 2 + len(shape)], axis=1 + axis).reshape(shape)


def kernel(
    sizes, al_ref, rs_hbm, lk_hbm, v_hbm,
    sol_ref, cor_ref, per_ref,
    rs_v, lk_v, vraw, v32, vall, relay, u8, lz, uz,
    res, total, hsum, tsend, trecv, zsend, zrecv, w_ref, ub_ref, g_ref, s_ref,
    cpart, csib, cmsg, cown, crecv, psend, precv, pwork,
    t_ss, t_rs, z_ss, z_rs, vh_ss, vh_rs, uh_ss, uh_rs, loc_s,
    o_ss, o_rs, r_ss, r_rs, b_ss, b_rs, c_ss, c_rs, p_ss, p_rs,
):
    n_grp, n_ta, n_xyz, scale = sizes
    grp = lax.axis_index("grp")
    ta = lax.axis_index("ta")
    me = lax.axis_index("xyz")
    chip, core = me // 2, me % 2
    n_chip = n_xyz // 2
    half_ta = n_ta // 2
    y = grp * 2 + ta // half_ta
    x = ta % half_ta

    def y_device(step):
        other = (y + step + 4) % 4
        return (other // 2, (other % 2) * half_ta + x, me)

    z_next = (grp, ta, (me + 1) % n_xyz)
    z_prev = (grp, ta, (me + n_xyz - 1) % n_xyz)
    t_next = (grp, (ta + 1) % n_ta, me)
    t_prev = (grp, (ta + n_ta - 1) % n_ta, me)

    barrier = pltpu.get_barrier_semaphore()
    for device in (y_device(1), y_device(-1), t_next, t_prev):
        pl.semaphore_signal(barrier, inc=1, device_id=device, device_id_type=MESH)

    @pl.loop(1, n_xyz)
    def _(o):
        pl.semaphore_signal(
            barrier, inc=1, device_id=(grp, ta, (me + o) % n_xyz), device_id_type=MESH
        )

    fetches = (
        pltpu.make_async_copy(lk_hbm, lk_v, loc_s.at[0]),
        pltpu.make_async_copy(rs_hbm, rs_v, loc_s.at[1]),
        pltpu.make_async_copy(v_hbm, vraw.at[0], loc_s.at[2]),
    )
    for copy in fetches:
        copy.start()

    def remote(src, dst, ss, rs, device):
        return pltpu.make_async_remote_copy(
            src_ref=src, dst_ref=dst, send_sem=ss, recv_sem=rs, device_id=device,
            device_id_type=MESH,
        )

    def way(c):
        return y_device(1 - 2 * (c % 2))

    def own_copy(c):
        rows = pl.ds(pl.multiple_of(c * 384, 384), 384)
        return remote(v_hbm.at[rows], relay.at[c], o_ss.at[c], o_rs.at[c], way(c))

    pl.semaphore_wait(barrier, n_xyz - 1 + 4)
    own_copy(0).start()
    own_copy(1).start()

    lane = lax.broadcasted_iota(jnp.int32, (8, 128), 1)
    sub = lax.broadcasted_iota(jnp.int32, (8, 128), 0)
    column = lane % SX
    z_is0 = sub % 2 == 0

    def shift_x(v, step):
        if step > 0:
            return jnp.where(column == SX - 1, roll(v, SX - 1, 1), roll(v, -1, 1))
        return jnp.where(column == 0, roll(v, 1 - SX, 1), roll(v, 1, 1))

    def shift_y(v, step):
        a = roll(v, -step * SX, 1)
        keep = lane < 128 - SX if step > 0 else lane >= SX
        return jnp.where(keep, a, roll(a, 4, 0))

    def spins(ref):
        v = ref[...].reshape(24, 8, 128)
        return [[v[6 * s + 3 * p : 6 * s + 3 * p + 3] for p in range(2)] for s in range(4)]

    def put(ref, s, p, value):
        k = 8 * (6 * s + 3 * p)
        ref[k : k + 24, :] = value.reshape(24, 128)

    def links_of(d):
        return u8[144 * d : 144 * (d + 1), :].reshape(2, 3, 3, 8, 128)

    def t_copies(n):
        return (
            remote(tsend.at[n, 0], trecv.at[n, 0], t_ss.at[n, 0], t_rs.at[n, 0], t_prev),
            remote(tsend.at[n, 1], trecv.at[n, 1], t_ss.at[n, 1], t_rs.at[n, 1], t_next),
            remote(zsend.at[n, 0], zrecv.at[n, 0], z_ss.at[n, 0], z_rs.at[n, 0], z_prev),
            remote(zsend.at[n, 1], zrecv.at[n, 1], z_ss.at[n, 1], z_rs.at[n, 1], z_next),
        )

    def prepare(n):
        psi = spins(res)

        def rows(re, im):
            both = jnp.stack([re, im])
            return both.reshape(both.size // 128, 128).astype(BF16)

        tsend[n, 0] = rows(*project(psi, 3, -1))
        tsend[n, 1] = rows(*colour(links_of(3), *project(psi, 3, 1), True))
        re, im = project(psi, 2, -1)
        zsend[n, 0] = rows(
            jnp.where(z_is0, re[0], roll(re[1], 1, 0)), jnp.where(z_is0, im[0], roll(im[1], 1, 0))
        )
        re, im = colour(links_of(2), *project(psi, 2, 1), True)
        zsend[n, 1] = rows(
            jnp.where(z_is0, roll(re[1], 7, 0), re[0]), jnp.where(z_is0, roll(im[1], 7, 0), im[0])
        )

    def local_hops():
        psi = spins(res)
        acc = [[None, None] for _ in range(4)]
        for d, shift in ((0, shift_x), (1, shift_y)):
            re, im = project(psi, d, -1)
            rebuild(acc, *colour(links_of(d), shift(re, 1), shift(im, 1), False), d, -1)
            re, im = colour(links_of(d), *project(psi, d, 1), True)
            rebuild(acc, shift(re, -1), shift(im, -1), d, 1)
        for s in range(4):
            for p in range(2):
                put(hsum, s, p, acc[s][p])

    def finish(n):
        psi = spins(res)
        acc = spins(hsum)
        sums = spins(total)
        sign_up = jnp.where(ta == n_ta - 1, -1.0, 1.0).astype(F32)
        sign_down = jnp.where(ta == 0, -1.0, 1.0).astype(F32)
        from_z = [zrecv[n, k].astype(F32).reshape(2, 3, 8, 128) for k in range(2)]
        from_t = [trecv[n, k].astype(F32).reshape(2, 2, 3, 8, 128) for k in range(2)]
        re, im = project(psi, 2, -1)

        def ahead(v, got):
            return jnp.where(z_is0, roll(v, 7, 0), jnp.stack([roll(got, 1, 0), got]))

        re, im = ahead(re, from_z[0][0]), ahead(im, from_z[0][1])
        rebuild(acc, *colour(links_of(2), re, im, False), 2, -1)
        re, im = colour(links_of(2), *project(psi, 2, 1), True)

        def behind(v, got):
            return jnp.where(z_is0, jnp.stack([roll(got, 7, 0), got]), roll(v, 1, 0))

        re, im = behind(re, from_z[1][0]), behind(im, from_z[1][1])
        rebuild(acc, re, im, 2, 1)
        re, im = from_t[0][0] * sign_up, from_t[0][1] * sign_up
        rebuild(acc, *colour(links_of(3), re, im, False), 3, -1)
        rebuild(acc, from_t[1][0] * sign_down, from_t[1][1] * sign_down, 3, 1)
        step = al_ref[n]
        step_after = al_ref[n + 1]
        for s in range(4):
            for p in range(2):
                old = psi[s][p]
                new = old - step * (old - HOPPING * acc[s][p])
                put(res, s, p, new)
                put(total, s, p, sums[s][p] + step_after * new)

    vall[256:352, :] = jnp.zeros((96, 3072), BF16)

    fetches[0].wait()
    fetches[1].wait()
    first_step = al_ref[0]
    for h in range(2):
        for z in range(2):
            links = lk_v[pl.ds(2 * h + z, 72, stride=4), :]
            for r in range(2):
                u8[pl.ds(4 * h + 2 * r + z, 72, stride=8), :] = links
                values = rs_v[pl.ds(96 * r + 2 * h + z, 24, stride=4), :]
                res[pl.ds(4 * h + 2 * r + z, 24, stride=8), :] = values
                total[pl.ds(4 * h + 2 * r + z, 24, stride=8), :] = first_step * values
            for d in range(3):
                rows = 0.5 * lk_v[pl.ds(72 * d + 2 * h + z, 18, stride=4), :]
                lz[z, d, :, 128 * h : 128 * (h + 1)] = rows
                if d == 2 and z == 1:
                    uz[:, 128 * h : 128 * (h + 1)] = rows
                if d == 2 and z == 0:
                    ub_ref[1, 2, :, 128 * h : 128 * (h + 1)] = rows
    lcol = lax.broadcasted_iota(jnp.int32, (18, 256), 1) % SX
    for z in range(2):
        links = lz[z, 0]
        ub_ref[z, 0] = jnp.where(
            lcol == 0, pltpu.roll(links, 256 - (SX - 1), axis=1), pltpu.roll(links, 1, axis=1)
        )
        ub_ref[z, 1] = pltpu.roll(lz[z, 1], SX, axis=1)

    def relay_copy(c):
        rows = pl.ds(pl.multiple_of(c * 384, 384), 384)
        return remote(relay.at[c], vraw.at[1, rows], r_ss.at[c], r_rs.at[c], way(c))

    def pass_on(step):
        for c in (2 * step, 2 * step + 1):
            own_copy(c).wait()
            relay_copy(c).start()

    def sort_chunk(which, c):
        v32[...] = vraw[which, pl.ds(pl.multiple_of(c * 384, 384), 384), :].astype(F32)
        rows = pl.ds(pl.multiple_of(which * 128 + c * 16, 16), 16)
        for m in range(6):
            for h in range(2):
                for z in range(2):
                    k = (z * 6 + m) * 256 + h * 128
                    vall[rows, k : k + 128] = v32[
                        pl.ds(4 * m + 2 * h + z, 16, stride=24), :
                    ].astype(BF16)

    own = pl.ds(0, 128)
    low, high = vall.at[own, pl.ds(0, 1536)], vall.at[own, pl.ds(1536, 1536)]
    halo_copies = (
        remote(low, w_ref.at[1, 0], vh_ss.at[0], vh_rs.at[0], z_prev),
        remote(high, w_ref.at[0, 1], vh_ss.at[1], vh_rs.at[1], z_next),
        remote(uz, ub_ref.at[0, 2], uh_ss, uh_rs, z_next),
        pltpu.make_async_copy(high, w_ref.at[0, 0], loc_s.at[0]),
        pltpu.make_async_copy(low, w_ref.at[1, 1], loc_s.at[1]),
    )

    def gradient(d):
        @pl.loop(0, 4)
        def _(q):
            z, h = q // 2, q % 2
            lanes = pl.ds(pl.multiple_of(h * 128, 128), 128)
            lane16 = lax.broadcasted_iota(jnp.int32, (16, 128), 1)

            def part(m, side=h):
                return pl.ds(pl.multiple_of(m * 256 + side * 128, 128), 128)

            @pl.loop(0, 8, unroll=4)
            def _(kc):
                rows = pl.ds(pl.multiple_of(kc * 16, 16), 16)

                def here(m, side):
                    return vall[rows, part(z * 6 + m, side)]

                def neighbours(m):
                    if d == 0:
                        v = here(m, h)
                        column = lane16 % SX
                        return (
                            jnp.where(
                                column == SX - 1,
                                pltpu.roll(v, SX - 1, axis=1),
                                pltpu.roll(v, 127, axis=1),
                            ),
                            jnp.where(
                                column == 0,
                                pltpu.roll(v, 129 - SX, axis=1),
                                pltpu.roll(v, 1, axis=1),
                            ),
                        )
                    if d == 1:
                        v, w = here(m, h), here(m, 1 - h)
                        up, down = 128 - SX, SX
                        return (
                            jnp.where(
                                lane16 < up,
                                pltpu.roll(v, up, axis=1),
                                pltpu.roll(w, up, axis=1),
                            ),
                            jnp.where(
                                lane16 >= down,
                                pltpu.roll(v, down, axis=1),
                                pltpu.roll(w, down, axis=1),
                            ),
                        )
                    return tuple(w_ref[z, s, rows, part(m)] for s in range(2))

                both = [neighbours(m) for m in range(6)]
                outs = []
                for side in range(2):
                    v = [both[m][side].astype(F32) for m in range(6)]
                    l_ref = lz if side == 0 else ub_ref
                    u = [
                        jnp.broadcast_to(l_ref[z, d, i : i + 1, lanes], (16, 128))
                        for i in range(18)
                    ]
                    for a in range(3):
                        re = im = None
                        for b in range(3):
                            if side == 0:
                                ur, ui = u[3 * a + b], u[9 + 3 * a + b]
                                t0 = ur * v[b] - ui * v[3 + b]
                                t1 = ur * v[3 + b] + ui * v[b]
                            else:
                                ur, ui = u[3 * b + a], u[9 + 3 * b + a]
                                t0 = ur * v[b] + ui * v[3 + b]
                                t1 = ur * v[3 + b] - ui * v[b]
                            re = t0 if re is None else re + t0
                            im = t1 if im is None else im + t1
                        outs.append((re, im))
                above = pl.ds(pl.multiple_of(d * 256 + kc * 16, 16), 16)
                below = pl.ds(pl.multiple_of(d * 256 + 128 + kc * 16, 16), 16)
                for a in range(3):
                    re = (outs[a][0] - outs[3 + a][0]).astype(BF16)
                    im = (outs[a][1] - outs[3 + a][1]).astype(BF16)
                    g_ref[above, part(z * 6 + a)] = re
                    g_ref[above, part(z * 6 + 3 + a)] = im
                    g_ref[below, part(z * 6 + a)] = im
                    g_ref[below, part(z * 6 + 3 + a)] = -re

    def sibling_copy(k, i):
        return remote(
            cpart.at[2 * k + 1 - core], csib.at[i], b_ss.at[i], b_rs.at[i],
            (grp, ta, me + 1 - 2 * core),
        )

    def c_copy(i):
        o = (i - chip + n_chip) % n_chip
        return remote(
            cmsg.at[i], crecv.at[o], c_ss.at[o], c_rs.at[o], (grp, ta, 2 * i + core)
        )

    def p_copy(target, o):
        return remote(
            psend.at[target], precv.at[o], p_ss.at[o], p_rs.at[o], (grp, ta, target)
        )

    def correlate(vectors, first, count):
        for d in range(3):
            c = dot_nt(g_ref[256 * d : 256 * (d + 1), :], vectors).T
            cpart[:, :, 256 * d : 256 * (d + 1)] = c.reshape(8, 16, 256)

        @pl.loop(0, count // 2)
        def _(k):
            sibling_copy(k, first // 2 + k).start()

    def combine(first, count):
        @pl.loop(0, count // 2)
        def _(k):
            i = first // 2 + k
            sibling_copy(k, i).wait()
            both = cpart[2 * k + core] + csib[i]

            @pl.when(i == chip)
            def _():
                cown[...] = both

            @pl.when(i != chip)
            def _():
                cmsg[i] = both.astype(BF16)
                c_copy(i).start()

    def overlap(vectors, first, count):
        p = dot_nt(vectors, s_ref[...]).reshape(16, 8, 128)
        p = jnp.where((lane // 16 == sub)[None], p, 0.0)
        p = jnp.sum(p, axis=1, keepdims=True)
        pwork[...] = p.reshape(8, 2, 1, 128)

        @pl.loop(0, count)
        def _(k):
            target = first + k
            o = (target - me + n_xyz) % n_xyz
            psend[target] = pwork[k]

            @pl.when(o != 0)
            def _():
                p_copy(target, o).start()

    @pl.loop(0, ITERS - 1)
    def _(n):
        prepare(n)
        for copy in t_copies(n):
            copy.start()

        @pl.when(n > 0)
        def _():
            pass_on(n - 1)

        @pl.when(n == 0)
        def _():
            @pl.loop(2, 8)
            def _(i):
                own_copy(i).start()

        local_hops()

        @pl.when(n == 0)
        def _():
            fetches[2].wait()

            @pl.loop(0, 8)
            def _(c):
                sort_chunk(0, c)

            for copy in halo_copies:
                copy.start()

            gradient(0)

        @pl.when(n == 1)
        def _():
            gradient(1)

        @pl.when(n == 2)
        def _():
            for copy in halo_copies:
                copy.wait()
            gradient(2)
            pass_on(2)
            correlate(vall[0:128, :], grp * 8, 8)
            pass_on(3)
            combine(grp * 8, 8)

        for copy in t_copies(n):
            copy.wait()
        finish(n)

    row = lax.broadcasted_iota(jnp.int32, (96, 48), 0)
    col = lax.broadcasted_iota(jnp.int32, (96, 48), 1)
    row_m, row_r, row_p, row_s = row // 16, (row // 8) % 2, (row // 4) % 2, row % 4
    col_r, col_s, col_m = col // 24, (col // 6) % 4, col % 6
    same = (row_r == col_r) & (row_s == col_s)
    want = jnp.where(row_p == 0, row_m, (row_m + 3) % 6)
    value = jnp.where((row_p == 1) & (row_m >= 3), -1.0, 1.0)
    pick = jnp.where(same & (want == col_m), value, 0.0).astype(BF16)
    for z in range(2):
        rows = []
        for r in range(2):
            halves = []
            for h in range(2):
                here = pl.ds(4 * h + 2 * r + z, 24, stride=8)
                there = pl.ds(96 * r + 2 * h + z, 24, stride=4)
                values = total[here, :]
                sol_ref[there, :] = values
                halves.append(values)
            rows.append(jnp.concatenate(halves, axis=1))
        spinors = jnp.concatenate(rows, axis=0).astype(BF16)
        placed = jnp.dot(pick, spinors, preferred_element_type=F32).astype(BF16)
        for m in range(6):
            rows = placed[16 * m : 16 * m + 16]
            s_ref[:, (z * 6 + m) * 256 : (z * 6 + m + 1) * 256] = jnp.concatenate([rows] * 8)

    overlap(vall[0:128, :], grp * 8, 8)

    @pl.loop(0, 2)
    def _(late):
        start, count = 6 * late, 6 - 4 * late

        @pl.loop(start, start + count)
        def _(c):
            relay_copy(c).wait()
            sort_chunk(1, c)

        first = (1 - grp) * 8 + start
        vectors = vall[pl.ds(pl.multiple_of(128 + 96 * late, 32), 128), :]
        correlate(vectors, first, count)
        overlap(vectors, first, count)
        combine(first, count)

    @pl.loop(1, n_xyz)
    def _(o):
        p_copy((me + o) % n_xyz, o).wait()

    @pl.loop(1, n_chip)
    def _(o):
        c_copy((chip + o) % n_chip).wait()

    c_sum = cown[...]
    for o in range(1, n_chip):
        c_sum = c_sum + crecv[o].astype(F32)
    p_sum = psend[me]
    for o in range(1, n_xyz):
        p_sum = p_sum + precv[o]
    for k in range(6):
        cor_ref[pl.ds(k, 16, stride=6), :] = c_sum[:, 128 * k : 128 * (k + 1)] * scale
    p_sum = p_sum * scale
    tall = []
    for i in range(2):
        wide = jnp.broadcast_to(p_sum[i], (8, 128))
        rows = wide
        for j in range(1, 8):
            rows = jnp.where(sub == j, pltpu.roll(wide, 128 - 16 * j, axis=1), rows)
        tall.append(rows)
    wide = jnp.concatenate(tall + [jnp.zeros((112, 128), F32)], axis=0).T
    per_ref[0] = wide[0:8, 0:16]
    per_ref[1] = wide[8:16, 0:16]


def rows_of(array, lead):
    return array.reshape(lead, 2, 2, 128).transpose(0, 2, 1, 3).reshape(lead * 4, 128)


def body(sizes, right_sides, gauge_links, eigenvectors, step_lengths):
    vmem = pl.BlockSpec(memory_space=pltpu.VMEM)
    anywhere = pl.BlockSpec(memory_space=pl.ANY)
    n_it = ITERS - 1
    dma = pltpu.SemaphoreType.DMA
    sol, cor, per = pl.pallas_call(
        functools.partial(kernel, sizes),
        out_shape=(
            pltpu.VMEM((192, 128), F32),
            pltpu.VMEM((96, 128), F32),
            pltpu.VMEM((2, 8, 16), F32),
        ),
        in_specs=[pl.BlockSpec(memory_space=pltpu.SMEM), anywhere, anywhere, anywhere],
        out_specs=(vmem, vmem, vmem),
        scratch_shapes=[
            pltpu.VMEM((192, 128), F32),
            pltpu.VMEM((288, 128), F32),
            pltpu.VMEM((2, 3072, 128), BF16),
            pltpu.VMEM((384, 128), F32),
            pltpu.VMEM((352, 3072), BF16),
            pltpu.VMEM((8, 384, 128), BF16),
            pltpu.VMEM((576, 128), F32),
            pltpu.VMEM((2, 3, 18, 256), F32),
            pltpu.VMEM((18, 256), F32),
            pltpu.VMEM((192, 128), F32),
            pltpu.VMEM((192, 128), F32),
            pltpu.VMEM((192, 128), F32),
            pltpu.VMEM((n_it, 2, 96, 128), BF16),
            pltpu.VMEM((n_it, 2, 96, 128), BF16),
            pltpu.VMEM((n_it, 2, 48, 128), BF16),
            pltpu.VMEM((n_it, 2, 48, 128), BF16),
            pltpu.VMEM((2, 2, 128, 1536), BF16),
            pltpu.VMEM((2, 3, 18, 256), F32),
            pltpu.VMEM((768, 3072), BF16),
            pltpu.VMEM((128, 3072), BF16),
            pltpu.VMEM((8, 16, 768), F32),
            pltpu.VMEM((8, 16, 768), F32),
            pltpu.VMEM((8, 16, 768), BF16),
            pltpu.VMEM((16, 768), F32),
            pltpu.VMEM((8, 16, 768), BF16),
            pltpu.VMEM((16, 2, 1, 128), F32),
            pltpu.VMEM((16, 2, 1, 128), F32),
            pltpu.VMEM((8, 2, 1, 128), F32),
            dma((n_it, 2)), dma((n_it, 2)), dma((n_it, 2)), dma((n_it, 2)),
            dma((2,)), dma((2,)), dma(()), dma(()), dma((3,)),
            dma((8,)), dma((8,)), dma((8,)), dma((8,)),
            dma((8,)), dma((8,)), dma((8,)), dma((8,)), dma((16,)), dma((16,)),
        ],
        compiler_params=pltpu.CompilerParams(
            collective_id=0, has_side_effects=True, vmem_limit_bytes=56 * 1024 * 1024
        ),
    )(
        step_lengths,
        rows_of(right_sides, 48),
        rows_of(gauge_links, 72),
        rows_of(eigenvectors, 768),
    )
    sol = sol.reshape(48, 2, 2, 128).transpose(0, 2, 1, 3).reshape(right_sides.shape)
    cor = cor.reshape(1, 16, 3, 2, 128)
    return sol, cor, per.transpose(2, 0, 1)[None]


def solution(mesh):
    n_grp, n_ta, n_xyz = (mesh.shape[a] for a in ("grp", "ta", "xyz"))
    scale = 1.0 / math.sqrt(2 * n_xyz * 256)
    return jax.shard_map(
        functools.partial(body, (n_grp, n_ta, n_xyz, scale)),
        mesh=mesh,
        in_specs=(
            P("grp", None, "ta", "xyz", None),
            P(None, None, "ta", "xyz", None),
            P("ta", "grp", None, "xyz", None),
            P(),
        ),
        out_specs=(
            P("grp", None, "ta", "xyz", None),
            P("ta", "xyz", None, None, "grp"),
            P("ta", "xyz", "grp", None),
        ),
        check_vma=False,
    )
```

```python
import functools
import math

import jax
import jax.numpy as jnp
from jax import lax
from jax.experimental import pallas as pl
from jax.experimental.pallas import tpu as pltpu
from jax.sharding import PartitionSpec as P

MESH = pl.DeviceIdType.MESH
F32 = jnp.float32
BF16 = jnp.bfloat16
SX = 16
ITERS = 4
HOPPING = 0.1
GAMMA_TABLE = (
    ((3, 0, 1), (2, 0, 1), (1, 0, -1), (0, 0, -1)),
    ((3, -1, 0), (2, 1, 0), (1, 1, 0), (0, -1, 0)),
    ((2, 0, 1), (3, 0, -1), (0, 0, -1), (1, 0, 1)),
    ((2, 1, 0), (3, 1, 0), (0, 1, 0), (1, 1, 0)),
)


def dot_nt(a, b):
    return lax.dot_general(a, b, (((1,), (1,)), ((), ())), preferred_element_type=F32)


def plus(a, b, sign):
    return a + b if sign > 0 else a - b


def phased(re, im, pr, pi):
    if pi == 0:
        return (pr, re), (pr, im)
    return (-pi, im), (pi, re)


def project(psi, direction, sign):
    re, im = [], []
    for target in range(2):
        source, pr, pi = GAMMA_TABLE[direction][target]
        (s0, a0), (s1, a1) = phased(psi[source][0], psi[source][1], pr, pi)
        re.append(plus(psi[target][0], a0, sign * s0))
        im.append(plus(psi[target][1], a1, sign * s1))
    return jnp.stack(re), jnp.stack(im)


def rebuild(acc, re, im, direction, sign):
    for target in range(4):
        if target < 2:
            terms = ((1, re[target]), (1, im[target]))
        else:
            source, pr, pi = GAMMA_TABLE[direction][target]
            (s0, a0), (s1, a1) = phased(re[source], im[source], pr, pi)
            terms = ((sign * s0, a0), (sign * s1, a1))
        for part in range(2):
            s, a = terms[part]
            old = acc[target][part]
            if old is None:
                acc[target][part] = a if s > 0 else -a
            else:
                acc[target][part] = plus(old, a, s)


def colour(u, re, im, dagger):
    out_re = out_im = None
    for b in range(3):
        ur = u[0, b] if dagger else u[0, :, b]
        ui = u[1, b] if dagger else u[1, :, b]
        vr, vi = re[:, b][:, None], im[:, b][:, None]
        ur, ui = ur[None], ui[None]
        t0 = plus(ur * vr, ui * vi, 1 if dagger else -1)
        t1 = plus(ur * vi, ui * vr, -1 if dagger else 1)
        out_re = t0 if out_re is None else out_re + t0
        out_im = t1 if out_im is None else out_im + t1
    return out_re, out_im


def roll(v, shift, axis):
    shape = v.shape
    flat = v.reshape((-1,) + shape[-2:])
    return pltpu.roll(flat, shift % shape[axis - 2 + len(shape)], axis=1 + axis).reshape(shape)


def kernel(
    sizes, al_ref, rs_hbm, lk_hbm, v_hbm,
    sol_ref, cor_ref, per_ref,
    rs_v, lk_v, vraw, v32, vall, relay, u8, lz, uz,
    res, total, hsum, tsend, trecv, zsend, zrecv, w_ref, ub_ref, g_ref, s_ref,
    cpart, csib, cmsg, cown, crecv, psend, precv, pwork,
    t_ss, t_rs, z_ss, z_rs, vh_ss, vh_rs, uh_ss, uh_rs, loc_s,
    o_ss, o_rs, r_ss, r_rs, b_ss, b_rs, c_ss, c_rs, p_ss, p_rs,
):
    n_grp, n_ta, n_xyz, scale = sizes
    grp = lax.axis_index("grp")
    ta = lax.axis_index("ta")
    me = lax.axis_index("xyz")
    chip, core = me // 2, me % 2
    n_chip = n_xyz // 2
    half_ta = n_ta // 2
    y = grp * 2 + ta // half_ta
    x = ta % half_ta

    def y_device(step):
        other = (y + step + 4) % 4
        return (other // 2, (other % 2) * half_ta + x, me)

    z_next = (grp, ta, (me + 1) % n_xyz)
    z_prev = (grp, ta, (me + n_xyz - 1) % n_xyz)
    t_next = (grp, (ta + 1) % n_ta, me)
    t_prev = (grp, (ta + n_ta - 1) % n_ta, me)

    barrier = pltpu.get_barrier_semaphore()
    for device in (y_device(1), y_device(-1), t_next, t_prev):
        pl.semaphore_signal(barrier, inc=1, device_id=device, device_id_type=MESH)

    @pl.loop(1, n_xyz)
    def _(o):
        pl.semaphore_signal(
            barrier, inc=1, device_id=(grp, ta, (me + o) % n_xyz), device_id_type=MESH
        )

    fetches = (
        pltpu.make_async_copy(lk_hbm, lk_v, loc_s.at[0]),
        pltpu.make_async_copy(rs_hbm, rs_v, loc_s.at[1]),
        pltpu.make_async_copy(v_hbm, vraw.at[0], loc_s.at[2]),
    )
    for copy in fetches:
        copy.start()

    def remote(src, dst, ss, rs, device):
        return pltpu.make_async_remote_copy(
            src_ref=src, dst_ref=dst, send_sem=ss, recv_sem=rs, device_id=device,
            device_id_type=MESH,
        )

    def way(c):
        return y_device(1 - 2 * (c % 2))

    def own_copy(c):
        rows = pl.ds(pl.multiple_of(c * 384, 384), 384)
        return remote(v_hbm.at[rows], relay.at[c], o_ss.at[c], o_rs.at[c], way(c))

    pl.semaphore_wait(barrier, n_xyz - 1 + 4)
    own_copy(0).start()
    own_copy(1).start()

    lane = lax.broadcasted_iota(jnp.int32, (8, 128), 1)
    sub = lax.broadcasted_iota(jnp.int32, (8, 128), 0)
    column = lane % SX
    z_is0 = sub % 2 == 0

    def shift_x(v, step):
        if step > 0:
            return jnp.where(column == SX - 1, roll(v, SX - 1, 1), roll(v, -1, 1))
        return jnp.where(column == 0, roll(v, 1 - SX, 1), roll(v, 1, 1))

    def shift_y(v, step):
        a = roll(v, -step * SX, 1)
        keep = lane < 128 - SX if step > 0 else lane >= SX
        return jnp.where(keep, a, roll(a, 4, 0))

    def spins(ref):
        v = ref[...].reshape(24, 8, 128)
        return [[v[6 * s + 3 * p : 6 * s + 3 * p + 3] for p in range(2)] for s in range(4)]

    def put(ref, s, p, value):
        k = 8 * (6 * s + 3 * p)
        ref[k : k + 24, :] = value.reshape(24, 128)

    def links_of(d):
        return u8[144 * d : 144 * (d + 1), :].reshape(2, 3, 3, 8, 128)

    def t_copies(n):
        return (
            remote(tsend.at[n, 0], trecv.at[n, 0], t_ss.at[n, 0], t_rs.at[n, 0], t_prev),
            remote(tsend.at[n, 1], trecv.at[n, 1], t_ss.at[n, 1], t_rs.at[n, 1], t_next),
            remote(zsend.at[n, 0], zrecv.at[n, 0], z_ss.at[n, 0], z_rs.at[n, 0], z_prev),
            remote(zsend.at[n, 1], zrecv.at[n, 1], z_ss.at[n, 1], z_rs.at[n, 1], z_next),
        )

    def prepare(n):
        psi = spins(res)

        def rows(re, im):
            both = jnp.stack([re, im])
            return both.reshape(both.size // 128, 128).astype(BF16)

        tsend[n, 0] = rows(*project(psi, 3, -1))
        tsend[n, 1] = rows(*colour(links_of(3), *project(psi, 3, 1), True))
        re, im = project(psi, 2, -1)
        zsend[n, 0] = rows(
            jnp.where(z_is0, re[0], roll(re[1], 1, 0)), jnp.where(z_is0, im[0], roll(im[1], 1, 0))
        )
        re, im = colour(links_of(2), *project(psi, 2, 1), True)
        zsend[n, 1] = rows(
            jnp.where(z_is0, roll(re[1], 7, 0), re[0]), jnp.where(z_is0, roll(im[1], 7, 0), im[0])
        )

    def local_hops():
        psi = spins(res)
        acc = [[None, None] for _ in range(4)]
        for d, shift in ((0, shift_x), (1, shift_y)):
            re, im = project(psi, d, -1)
            rebuild(acc, *colour(links_of(d), shift(re, 1), shift(im, 1), False), d, -1)
            re, im = colour(links_of(d), *project(psi, d, 1), True)
            rebuild(acc, shift(re, -1), shift(im, -1), d, 1)
        for s in range(4):
            for p in range(2):
                put(hsum, s, p, acc[s][p])

    def finish(n):
        psi = spins(res)
        acc = spins(hsum)
        sums = spins(total)
        sign_up = jnp.where(ta == n_ta - 1, -1.0, 1.0).astype(F32)
        sign_down = jnp.where(ta == 0, -1.0, 1.0).astype(F32)
        from_z = [zrecv[n, k].astype(F32).reshape(2, 3, 8, 128) for k in range(2)]
        from_t = [trecv[n, k].astype(F32).reshape(2, 2, 3, 8, 128) for k in range(2)]
        re, im = project(psi, 2, -1)

        def ahead(v, got):
            return jnp.where(z_is0, roll(v, 7, 0), jnp.stack([roll(got, 1, 0), got]))

        re, im = ahead(re, from_z[0][0]), ahead(im, from_z[0][1])
        rebuild(acc, *colour(links_of(2), re, im, False), 2, -1)
        re, im = colour(links_of(2), *project(psi, 2, 1), True)

        def behind(v, got):
            return jnp.where(z_is0, jnp.stack([roll(got, 7, 0), got]), roll(v, 1, 0))

        re, im = behind(re, from_z[1][0]), behind(im, from_z[1][1])
        rebuild(acc, re, im, 2, 1)
        re, im = from_t[0][0] * sign_up, from_t[0][1] * sign_up
        rebuild(acc, *colour(links_of(3), re, im, False), 3, -1)
        rebuild(acc, from_t[1][0] * sign_down, from_t[1][1] * sign_down, 3, 1)
        step = al_ref[n]
        step_after = al_ref[n + 1]
        for s in range(4):
            for p in range(2):
                old = psi[s][p]
                new = old - step * (old - HOPPING * acc[s][p])
                put(res, s, p, new)
                put(total, s, p, sums[s][p] + step_after * new)

    vall[256:352, :] = jnp.zeros((96, 3072), BF16)

    fetches[0].wait()
    fetches[1].wait()
    first_step = al_ref[0]
    for h in range(2):
        for z in range(2):
            links = lk_v[pl.ds(2 * h + z, 72, stride=4), :]
            for r in range(2):
                u8[pl.ds(4 * h + 2 * r + z, 72, stride=8), :] = links
                values = rs_v[pl.ds(96 * r + 2 * h + z, 24, stride=4), :]
                res[pl.ds(4 * h + 2 * r + z, 24, stride=8), :] = values
                total[pl.ds(4 * h + 2 * r + z, 24, stride=8), :] = first_step * values
            for d in range(3):
                rows = 0.5 * lk_v[pl.ds(72 * d + 2 * h + z, 18, stride=4), :]
                lz[z, d, :, 128 * h : 128 * (h + 1)] = rows
                if d == 2 and z == 1:
                    uz[:, 128 * h : 128 * (h + 1)] = rows
                if d == 2 and z == 0:
                    ub_ref[1, 2, :, 128 * h : 128 * (h + 1)] = rows
    lcol = lax.broadcasted_iota(jnp.int32, (18, 256), 1) % SX
    for z in range(2):
        links = lz[z, 0]
        ub_ref[z, 0] = jnp.where(
            lcol == 0, pltpu.roll(links, 256 - (SX - 1), axis=1), pltpu.roll(links, 1, axis=1)
        )
        ub_ref[z, 1] = pltpu.roll(lz[z, 1], SX, axis=1)

    def relay_copy(c):
        rows = pl.ds(pl.multiple_of(c * 384, 384), 384)
        return remote(relay.at[c], vraw.at[1, rows], r_ss.at[c], r_rs.at[c], way(c))

    def pass_on(step):
        for c in (2 * step, 2 * step + 1):
            own_copy(c).wait()
            relay_copy(c).start()

    def sort_chunk(which, c):
        v32[...] = vraw[which, pl.ds(pl.multiple_of(c * 384, 384), 384), :].astype(F32)
        rows = pl.ds(pl.multiple_of(which * 128 + c * 16, 16), 16)
        for m in range(6):
            for h in range(2):
                for z in range(2):
                    k = (z * 6 + m) * 256 + h * 128
                    vall[rows, k : k + 128] = v32[
                        pl.ds(4 * m + 2 * h + z, 16, stride=24), :
                    ].astype(BF16)

    own = pl.ds(0, 128)
    low, high = vall.at[own, pl.ds(0, 1536)], vall.at[own, pl.ds(1536, 1536)]
    halo_copies = (
        remote(low, w_ref.at[1, 0], vh_ss.at[0], vh_rs.at[0], z_prev),
        remote(high, w_ref.at[0, 1], vh_ss.at[1], vh_rs.at[1], z_next),
        remote(uz, ub_ref.at[0, 2], uh_ss, uh_rs, z_next),
        pltpu.make_async_copy(high, w_ref.at[0, 0], loc_s.at[0]),
        pltpu.make_async_copy(low, w_ref.at[1, 1], loc_s.at[1]),
    )

    def gradient(d):
        @pl.loop(0, 4)
        def _(q):
            z, h = q // 2, q % 2
            lanes = pl.ds(pl.multiple_of(h * 128, 128), 128)
            lane16 = lax.broadcasted_iota(jnp.int32, (16, 128), 1)

            def part(m, side=h):
                return pl.ds(pl.multiple_of(m * 256 + side * 128, 128), 128)

            @pl.loop(0, 8, unroll=4)
            def _(kc):
                rows = pl.ds(pl.multiple_of(kc * 16, 16), 16)

                def here(m, side):
                    return vall[rows, part(z * 6 + m, side)]

                def neighbours(m):
                    if d == 0:
                        v = here(m, h)
                        column = lane16 % SX
                        return (
                            jnp.where(
                                column == SX - 1,
                                pltpu.roll(v, SX - 1, axis=1),
                                pltpu.roll(v, 127, axis=1),
                            ),
                            jnp.where(
                                column == 0,
                                pltpu.roll(v, 129 - SX, axis=1),
                                pltpu.roll(v, 1, axis=1),
                            ),
                        )
                    if d == 1:
                        v, w = here(m, h), here(m, 1 - h)
                        up, down = 128 - SX, SX
                        return (
                            jnp.where(
                                lane16 < up,
                                pltpu.roll(v, up, axis=1),
                                pltpu.roll(w, up, axis=1),
                            ),
                            jnp.where(
                                lane16 >= down,
                                pltpu.roll(v, down, axis=1),
                                pltpu.roll(w, down, axis=1),
                            ),
                        )
                    return tuple(w_ref[z, s, rows, part(m)] for s in range(2))

                both = [neighbours(m) for m in range(6)]
                outs = []
                for side in range(2):
                    v = [both[m][side].astype(F32) for m in range(6)]
                    l_ref = lz if side == 0 else ub_ref
                    u = [
                        jnp.broadcast_to(l_ref[z, d, i : i + 1, lanes], (16, 128))
                        for i in range(18)
                    ]
                    for a in range(3):
                        re = im = None
                        for b in range(3):
                            if side == 0:
                                ur, ui = u[3 * a + b], u[9 + 3 * a + b]
                                t0 = ur * v[b] - ui * v[3 + b]
                                t1 = ur * v[3 + b] + ui * v[b]
                            else:
                                ur, ui = u[3 * b + a], u[9 + 3 * b + a]
                                t0 = ur * v[b] + ui * v[3 + b]
                                t1 = ur * v[3 + b] - ui * v[b]
                            re = t0 if re is None else re + t0
                            im = t1 if im is None else im + t1
                        outs.append((re, im))
                above = pl.ds(pl.multiple_of(d * 256 + kc * 16, 16), 16)
                below = pl.ds(pl.multiple_of(d * 256 + 128 + kc * 16, 16), 16)
                for a in range(3):
                    re = (outs[a][0] - outs[3 + a][0]).astype(BF16)
                    im = (outs[a][1] - outs[3 + a][1]).astype(BF16)
                    g_ref[above, part(z * 6 + a)] = re
                    g_ref[above, part(z * 6 + 3 + a)] = im
                    g_ref[below, part(z * 6 + a)] = im
                    g_ref[below, part(z * 6 + 3 + a)] = -re

    def sibling_copy(k, i):
        return remote(
            cpart.at[2 * k + 1 - core], csib.at[i], b_ss.at[i], b_rs.at[i],
            (grp, ta, me + 1 - 2 * core),
        )

    def c_copy(i):
        o = (i - chip + n_chip) % n_chip
        return remote(
            cmsg.at[i], crecv.at[o], c_ss.at[o], c_rs.at[o], (grp, ta, 2 * i + core)
        )

    def p_copy(target, o):
        return remote(
            psend.at[target], precv.at[o], p_ss.at[o], p_rs.at[o], (grp, ta, target)
        )

    def correlate(vectors, first, count):
        for d in range(3):
            c = dot_nt(g_ref[256 * d : 256 * (d + 1), :], vectors).T
            cpart[:, :, 256 * d : 256 * (d + 1)] = c.reshape(8, 16, 256)

        @pl.loop(0, count // 2)
        def _(k):
            sibling_copy(k, first // 2 + k).start()

    def combine(first, count):
        @pl.loop(0, count // 2)
        def _(k):
            i = first // 2 + k
            sibling_copy(k, i).wait()
            both = cpart[2 * k + core] + csib[i]

            @pl.when(i == chip)
            def _():
                cown[...] = both

            @pl.when(i != chip)
            def _():
                cmsg[i] = both.astype(BF16)
                c_copy(i).start()

    def overlap(vectors, first, count):
        p = dot_nt(vectors, s_ref[...]).reshape(16, 8, 128)
        p = jnp.where((lane // 16 == sub)[None], p, 0.0)
        p = jnp.sum(p, axis=1, keepdims=True)
        pwork[...] = p.reshape(8, 2, 1, 128)

        @pl.loop(0, count)
        def _(k):
            target = first + k
            o = (target - me + n_xyz) % n_xyz
            psend[target] = pwork[k]

            @pl.when(o != 0)
            def _():
                p_copy(target, o).start()

    @pl.loop(0, ITERS - 1)
    def _(n):
        prepare(n)
        for copy in t_copies(n):
            copy.start()

        @pl.when(n > 0)
        def _():
            pass_on(n - 1)

        @pl.when(n == 0)
        def _():
            @pl.loop(2, 8)
            def _(i):
                own_copy(i).start()

        local_hops()

        @pl.when(n == 0)
        def _():
            fetches[2].wait()

            @pl.loop(0, 8)
            def _(c):
                sort_chunk(0, c)

            for copy in halo_copies:
                copy.start()

            gradient(0)

        @pl.when(n == 1)
        def _():
            gradient(1)

        @pl.when(n == 2)
        def _():
            for copy in halo_copies:
                copy.wait()
            gradient(2)
            pass_on(2)
            correlate(vall[0:128, :], grp * 8, 8)
            pass_on(3)

        for copy in t_copies(n):
            copy.wait()
        finish(n)

    row = lax.broadcasted_iota(jnp.int32, (96, 48), 0)
    col = lax.broadcasted_iota(jnp.int32, (96, 48), 1)
    row_m, row_r, row_p, row_s = row // 16, (row // 8) % 2, (row // 4) % 2, row % 4
    col_r, col_s, col_m = col // 24, (col // 6) % 4, col % 6
    same = (row_r == col_r) & (row_s == col_s)
    want = jnp.where(row_p == 0, row_m, (row_m + 3) % 6)
    value = jnp.where((row_p == 1) & (row_m >= 3), -1.0, 1.0)
    pick = jnp.where(same & (want == col_m), value, 0.0).astype(BF16)
    for z in range(2):
        rows = []
        for r in range(2):
            halves = []
            for h in range(2):
                here = pl.ds(4 * h + 2 * r + z, 24, stride=8)
                there = pl.ds(96 * r + 2 * h + z, 24, stride=4)
                values = total[here, :]
                sol_ref[there, :] = values
                halves.append(values)
            rows.append(jnp.concatenate(halves, axis=1))
        spinors = jnp.concatenate(rows, axis=0).astype(BF16)
        placed = jnp.dot(pick, spinors, preferred_element_type=F32).astype(BF16)
        for m in range(6):
            rows = placed[16 * m : 16 * m + 16]
            s_ref[:, (z * 6 + m) * 256 : (z * 6 + m + 1) * 256] = jnp.concatenate([rows] * 8)

    overlap(vall[0:128, :], grp * 8, 8)
    combine(grp * 8, 8)

    @pl.loop(0, 2)
    def _(late):
        start, count = 6 * late, 6 - 4 * late

        @pl.loop(start, start + count)
        def _(c):
            relay_copy(c).wait()
            sort_chunk(1, c)

        first = (1 - grp) * 8 + start
        vectors = vall[pl.ds(pl.multiple_of(128 + 96 * late, 32), 128), :]
        correlate(vectors, first, count)
        overlap(vectors, first, count)
        combine(first, count)

    @pl.loop(1, n_xyz)
    def _(o):
        p_copy((me + o) % n_xyz, o).wait()

    @pl.loop(1, n_chip)
    def _(o):
        c_copy((chip + o) % n_chip).wait()

    c_sum = cown[...]
    for o in range(1, n_chip):
        c_sum = c_sum + crecv[o].astype(F32)
    p_sum = psend[me]
    for o in range(1, n_xyz):
        p_sum = p_sum + precv[o]
    for k in range(6):
        cor_ref[pl.ds(k, 16, stride=6), :] = c_sum[:, 128 * k : 128 * (k + 1)] * scale
    p_sum = p_sum * scale
    tall = []
    for i in range(2):
        wide = jnp.broadcast_to(p_sum[i], (8, 128))
        rows = wide
        for j in range(1, 8):
            rows = jnp.where(sub == j, pltpu.roll(wide, 128 - 16 * j, axis=1), rows)
        tall.append(rows)
    wide = jnp.concatenate(tall + [jnp.zeros((112, 128), F32)], axis=0).T
    per_ref[0] = wide[0:8, 0:16]
    per_ref[1] = wide[8:16, 0:16]


def rows_of(array, lead):
    return array.reshape(lead, 2, 2, 128).transpose(0, 2, 1, 3).reshape(lead * 4, 128)


def body(sizes, right_sides, gauge_links, eigenvectors, step_lengths):
    vmem = pl.BlockSpec(memory_space=pltpu.VMEM)
    anywhere = pl.BlockSpec(memory_space=pl.ANY)
    n_it = ITERS - 1
    dma = pltpu.SemaphoreType.DMA
    sol, cor, per = pl.pallas_call(
        functools.partial(kernel, sizes),
        out_shape=(
            pltpu.VMEM((192, 128), F32),
            pltpu.VMEM((96, 128), F32),
            pltpu.VMEM((2, 8, 16), F32),
        ),
        in_specs=[pl.BlockSpec(memory_space=pltpu.SMEM), anywhere, anywhere, anywhere],
        out_specs=(vmem, vmem, vmem),
        scratch_shapes=[
            pltpu.VMEM((192, 128), F32),
            pltpu.VMEM((288, 128), F32),
            pltpu.VMEM((2, 3072, 128), BF16),
            pltpu.VMEM((384, 128), F32),
            pltpu.VMEM((352, 3072), BF16),
            pltpu.VMEM((8, 384, 128), BF16),
            pltpu.VMEM((576, 128), F32),
            pltpu.VMEM((2, 3, 18, 256), F32),
            pltpu.VMEM((18, 256), F32),
            pltpu.VMEM((192, 128), F32),
            pltpu.VMEM((192, 128), F32),
            pltpu.VMEM((192, 128), F32),
            pltpu.VMEM((n_it, 2, 96, 128), BF16),
            pltpu.VMEM((n_it, 2, 96, 128), BF16),
            pltpu.VMEM((n_it, 2, 48, 128), BF16),
            pltpu.VMEM((n_it, 2, 48, 128), BF16),
            pltpu.VMEM((2, 2, 128, 1536), BF16),
            pltpu.VMEM((2, 3, 18, 256), F32),
            pltpu.VMEM((768, 3072), BF16),
            pltpu.VMEM((128, 3072), BF16),
            pltpu.VMEM((8, 16, 768), F32),
            pltpu.VMEM((8, 16, 768), F32),
            pltpu.VMEM((8, 16, 768), BF16),
            pltpu.VMEM((16, 768), F32),
            pltpu.VMEM((8, 16, 768), BF16),
            pltpu.VMEM((16, 2, 1, 128), F32),
            pltpu.VMEM((16, 2, 1, 128), F32),
            pltpu.VMEM((8, 2, 1, 128), F32),
            dma((n_it, 2)), dma((n_it, 2)), dma((n_it, 2)), dma((n_it, 2)),
            dma((2,)), dma((2,)), dma(()), dma(()), dma((3,)),
            dma((8,)), dma((8,)), dma((8,)), dma((8,)),
            dma((8,)), dma((8,)), dma((8,)), dma((8,)), dma((16,)), dma((16,)),
        ],
        compiler_params=pltpu.CompilerParams(
            collective_id=0, has_side_effects=True, vmem_limit_bytes=56 * 1024 * 1024
        ),
    )(
        step_lengths,
        rows_of(right_sides, 48),
        rows_of(gauge_links, 72),
        rows_of(eigenvectors, 768),
    )
    sol = sol.reshape(48, 2, 2, 128).transpose(0, 2, 1, 3).reshape(right_sides.shape)
    cor = cor.reshape(1, 16, 3, 2, 128)
    return sol, cor, per.transpose(2, 0, 1)[None]


def solution(mesh):
    n_grp, n_ta, n_xyz = (mesh.shape[a] for a in ("grp", "ta", "xyz"))
    scale = 1.0 / math.sqrt(2 * n_xyz * 256)
    return jax.shard_map(
        functools.partial(body, (n_grp, n_ta, n_xyz, scale)),
        mesh=mesh,
        in_specs=(
            P("grp", None, "ta", "xyz", None),
            P(None, None, "ta", "xyz", None),
            P("ta", "grp", None, "xyz", None),
            P(),
        ),
        out_specs=(
            P("grp", None, "ta", "xyz", None),
            P("ta", "xyz", None, None, "grp"),
            P("ta", "xyz", "grp", None),
        ),
        check_vma=False,
    )
```
